512 devices in a mesh: lon: 64 (over z_lo, x, y), lat: 8 (over z_hi, core).
Axes of the slice: x: 4, y: 8, z: 8 (z_hi: 4, z_lo: 2; z = z_hi * 2 + z_lo), core: 2. Of those that a mesh axis runs over, the one named last changes fastest.
Arguments:
- thermal_anomaly: float32 [16, 512, 1024], P(None, 'lon', 'lat'), may hold values from -6 to 6
- saltiness_anomaly: float32 [16, 512, 1024], P(None, 'lon', 'lat'), may hold values from -6 to 6
- zonal_current: float32 [16, 512, 1024], P(None, 'lon', 'lat'), may hold values from -3 to 3
- meridional_current: float32 [16, 512, 1024], P(None, 'lon', 'lat'), may hold values from -3 to 3
- bottom_ocean_layer: int32 [512, 1024], P('lon', 'lat'), may hold values from 0 to 16
- seam_axis_meridian: int32 [1], replicated, may hold values from 0 to 1023
- interface_diffusivity: float32 [15, 512, 1024], P(None, 'lon', 'lat'), may hold values from 0.1 to 10
- atmospheric_forcing: float32 [2, 512, 1024], P(None, 'lon', 'lat'), may hold values from -6 to 6
Outputs:
- temperature_next: float32 [16, 512, 1024], P(None, 'lon', 'lat')
- salinity_next: float32 [16, 512, 1024], P(None, 'lon', 'lat')
- zonal_next: float32 [16, 512, 1024], P(None, 'lon', 'lat')
- meridional_next: float32 [16, 512, 1024], P(None, 'lon', 'lat')
The draws below stay inside these ranges and needn't reach their ends.
Inputs may be any that keep to these rules, and one draw needn't show every extreme that they name: `seam_axis_meridian`: an even code folds about a cell centre, an odd one about a cell corner.
All inputs are finite; a program needn't handle non-finite values.
Results may differ from the reference program's by a relative error of at most 0.0003.
Values sent between devices are 32-bit elements; how exact they have to be, the bound alone decides.
A program may use at most 64 MiB of HBM per device.

```python
import math
import jax
import jax.numpy as jnp
from jax import lax

SEA_LAYERS = 16
CY = 128
PARALLEL_SPAN = 512
MERIDIAN_SPAN = 1024
N_LAT = 8


def banded_field(key, scale, bound, band_rows, band_low, band_high):
    field_shape = (SEA_LAYERS, PARALLEL_SPAN, MERIDIAN_SPAN)
    key_first, key_second, key_third = jax.random.split(key, 3)
    background = jnp.clip(scale * jax.random.normal(key_first, field_shape, jnp.float32), -bound, bound)
    magnitude = jax.random.uniform(key_second, field_shape, jnp.float32, band_low, band_high)
    sign_value = (2 * jax.random.randint(key_third, field_shape, 0, 2) - 1).astype(jnp.float32)
    row_index = jnp.arange(MERIDIAN_SPAN)
    in_band = (row_index >= MERIDIAN_SPAN - band_rows)[None, None, :]
    return jnp.where(in_band, sign_value * magnitude, background).astype(jnp.float32)


def draw_thermal_anomaly(key, part):
    return banded_field(jax.random.fold_in(key, 101), 1.0, 6.0, 4, 4.0, 6.0)


def draw_saltiness_anomaly(key, part):
    return banded_field(jax.random.fold_in(key, 202), 1.0, 6.0, 4, 4.0, 6.0)


def draw_meridional_current(key, part):
    return banded_field(jax.random.fold_in(key, 303), 0.5, 3.0, 3, 2.0, 3.0)


def set_ends(array, own_key, low, high):
    extent = array.shape
    index_at = [jax.random.randint(jax.random.fold_in(own_key, axis), (), 0, extent[axis]) for axis in range(len(extent))]
    array = array.at[tuple(index_at)].set(low)
    longest = extent.index(max(extent))
    index_at[longest] = (index_at[longest] + 1) % extent[longest]
    return array.at[tuple(index_at)].set(high)


def levels(key, dims, shards, least, largest):
    def one(dim, parts):
        heights = jax.random.uniform(jax.random.fold_in(jax.random.fold_in(key, 6), dim), (parts,), jnp.float32, least / len(shards), largest / len(shards))
        return jnp.repeat(jnp.exp(heights), dims[dim] // parts).reshape((-1,) + (1,) * (len(dims) - dim - 1))

    gain = one(*shards[0])
    for cut in shards[1:]:
        gain = gain * one(*cut)
    return gain


def bell_draw(stream_key, extent, width, reach, pieces=(), held_as=jnp.bfloat16):
    values = width * jax.random.normal(stream_key, extent, jnp.float32)
    if pieces:
        values = values * levels(stream_key, extent, pieces, -0.22, 0.18)
    return jnp.clip(values, -reach, reach).astype(held_as)


def setup_inputs(seed: int = 0) -> dict:
    seeds = jax.random.split(jax.random.key(seed), 9)
    thermal_anomaly = draw_thermal_anomaly(jax.random.fold_in(seeds[8], 71), 0)
    saltiness_anomaly = draw_saltiness_anomaly(jax.random.fold_in(seeds[8], 71), 0)
    zonal_current = bell_draw(seeds[2], (SEA_LAYERS, PARALLEL_SPAN, MERIDIAN_SPAN), 0.5, 3.0, ((1, 64), (2, 8)), jnp.float32)
    meridional_current = draw_meridional_current(jax.random.fold_in(seeds[8], 71), 0)
    bottom_ocean_layer = set_ends(jax.random.randint(seeds[4], (PARALLEL_SPAN, MERIDIAN_SPAN), 0, SEA_LAYERS + 1), jax.random.fold_in(seeds[4], 1), 0, SEA_LAYERS).astype(jnp.int32)
    seam_axis_meridian = jax.random.randint(seeds[5], (1,), 0, 2 * PARALLEL_SPAN).astype(jnp.int32)
    interface_diffusivity = jnp.clip(jnp.exp(math.log(10.0) - 4.6051702 * jax.random.uniform(seeds[6], (SEA_LAYERS - 1, PARALLEL_SPAN, MERIDIAN_SPAN), jnp.float32) ** levels(seeds[6], (SEA_LAYERS - 1, PARALLEL_SPAN, MERIDIAN_SPAN), ((1, 64), (2, 8)), -0.2, 0.2)), 0.1, 10.0)
    atmospheric_forcing = bell_draw(seeds[7], (2, PARALLEL_SPAN, MERIDIAN_SPAN), 1.0, 6.0, ((1, 64), (2, 8)), jnp.float32)
    return dict(thermal_anomaly=thermal_anomaly, saltiness_anomaly=saltiness_anomaly, zonal_current=zonal_current, meridional_current=meridional_current, bottom_ocean_layer=bottom_ocean_layer, seam_axis_meridian=seam_axis_meridian, interface_diffusivity=interface_diffusivity, atmospheric_forcing=atmospheric_forcing)


TIME_STEP = 0.2
TRACER_DIFF = 0.2
MOMENTUM_VISC = 0.2
THERMAL_EXPANSION = 0.5
HALINE_CONTRACTION = 0.4
WIND_GAIN = 2.0
VERTICAL_VISC = 1.0
NEIGHBOURS = ((1, 0), (-1, 0), (0, 1), (0, -1))


def implicit(right_side, coupling):
    count = right_side.shape[-3]
    ratios = []
    values = []
    for level_k in range(count):
        below = coupling[level_k] if level_k < count - 1 else 0.0
        above = coupling[level_k - 1] if level_k > 0 else 0.0
        if level_k == 0:
            denom = 1.0 + below
            values.append(right_side[..., 0, :, :] / denom)
        else:
            denom = 1.0 + above + below + above * ratios[level_k - 1]
            values.append((right_side[..., level_k, :, :] + above * values[level_k - 1]) / denom)
        ratios.append(-below / denom)
    result = [values[count - 1]]
    for level_k in range(count - 2, -1, -1):
        result.insert(0, values[level_k] - ratios[level_k] * result[0])
    return jnp.stack(result, axis=-3)


def choose_rows(source, fold_type, sign_column):
    upper = jnp.where(fold_type == 1, source[..., 2], source[..., 1])
    outer = jnp.where(fold_type == 1, source[..., 1], source[..., 0])
    return jnp.stack([upper, outer], axis=-1) * sign_column


def advance(grid_ext, interface_diffusivity, atmospheric_forcing, row_start, rows_total):
    layer_number = (grid_ext.shape[0] - 1) // 4
    cols_n = grid_ext.shape[1] - 4
    rows_n = grid_ext.shape[2] - 4

    def view(source_array, shift_x, shift_y):
        return source_array[..., 2 + shift_x:2 + shift_x + cols_n, 2 + shift_y:2 + shift_y + rows_n]

    tracers = grid_ext[:2 * layer_number].reshape(2, layer_number, cols_n + 4, rows_n + 4)
    zonal = grid_ext[2 * layer_number:3 * layer_number]
    merid = grid_ext[3 * layer_number:4 * layer_number]
    depth_count = grid_ext[4 * layer_number]
    level_ids = jnp.arange(layer_number).astype(jnp.float32)[:, None, None]
    wet_mask = jnp.where(level_ids < depth_count[None], 1.0, 0.0).astype(jnp.float32)

    def face_x(shift_x):
        interp = (7.0 * (view(tracers, shift_x, 0) + view(tracers, shift_x + 1, 0)) - (view(tracers, shift_x - 1, 0) + view(tracers, shift_x + 2, 0))) / 12.0
        return view(zonal, shift_x, 0) * view(wet_mask, shift_x, 0) * view(wet_mask, shift_x + 1, 0) * interp

    def face_y(shift_y):
        interp = (7.0 * (view(tracers, 0, shift_y) + view(tracers, 0, shift_y + 1)) - (view(tracers, 0, shift_y - 1) + view(tracers, 0, shift_y + 2))) / 12.0
        return view(merid, 0, shift_y) * view(wet_mask, 0, shift_y) * view(wet_mask, 0, shift_y + 1) * interp

    advect = -(face_x(0) - face_x(-1)) - (face_y(0) - face_y(-1))
    centre = view(tracers, 0, 0)
    wet_centre = view(wet_mask, 0, 0)
    spread = jnp.zeros_like(centre)
    for shift_x, shift_y in NEIGHBOURS:
        spread = spread + view(wet_mask, shift_x, shift_y) * wet_centre * (view(tracers, shift_x, shift_y) - centre)
    tracer_star = centre + TIME_STEP * (advect + TRACER_DIFF * spread) * wet_centre

    buoyancy = (THERMAL_EXPANSION * grid_ext[:layer_number] - HALINE_CONTRACTION * grid_ext[layer_number:2 * layer_number]) * wet_mask
    pressure = jnp.cumsum(buoyancy, axis=0) - 0.5 * buoyancy
    u_mask = wet_centre * view(wet_mask, 1, 0)
    v_mask = wet_centre * view(wet_mask, 0, 1)
    row_ids = (row_start + jnp.arange(rows_n)).astype(jnp.float32)
    cor_u = 2.0 * (row_ids + 0.5) / rows_total - 1.0
    cor_v = 2.0 * (row_ids + 1.0) / rows_total - 1.0
    v_at_u = 0.25 * (view(merid, 0, 0) + view(merid, 0, -1) + view(merid, 1, 0) + view(merid, 1, -1))
    u_at_v = 0.25 * (view(zonal, 0, 0) + view(zonal, -1, 0) + view(zonal, 0, 1) + view(zonal, -1, 1))
    u_centre = view(zonal, 0, 0)
    v_centre = view(merid, 0, 0)
    u_visc = jnp.zeros_like(u_centre)
    v_visc = jnp.zeros_like(v_centre)
    for shift_x, shift_y in NEIGHBOURS:
        u_visc = u_visc + view(wet_mask, shift_x, shift_y) * view(wet_mask, shift_x + 1, shift_y) * u_mask * (view(zonal, shift_x, shift_y) - u_centre)
        v_visc = v_visc + view(wet_mask, shift_x, shift_y) * view(wet_mask, shift_x, shift_y + 1) * v_mask * (view(merid, shift_x, shift_y) - v_centre)
    u_star = (u_centre + TIME_STEP * (cor_u * v_at_u - (view(pressure, 1, 0) - view(pressure, 0, 0)) + MOMENTUM_VISC * u_visc)) * u_mask
    v_star = (v_centre + TIME_STEP * (-cor_v * u_at_v - (view(pressure, 0, 1) - view(pressure, 0, 0)) + MOMENTUM_VISC * v_visc)) * v_mask
    u_star = u_star.at[0].add(TIME_STEP * WIND_GAIN * atmospheric_forcing[0] * u_mask[0])
    v_star = v_star.at[0].add(TIME_STEP * WIND_GAIN * atmospheric_forcing[1] * v_mask[0])

    tracer_next = implicit(tracer_star, TIME_STEP * interface_diffusivity * wet_centre[:-1] * wet_centre[1:])
    u_next = implicit(u_star, TIME_STEP * VERTICAL_VISC * u_mask[:-1] * u_mask[1:])
    v_next = implicit(v_star, TIME_STEP * VERTICAL_VISC * v_mask[:-1] * v_mask[1:])
    return tracer_next[0], tracer_next[1], u_next, v_next


def reference(thermal_anomaly, saltiness_anomaly, zonal_current, meridional_current, bottom_ocean_layer, seam_axis_meridian, interface_diffusivity, atmospheric_forcing):
    layer_number = thermal_anomaly.shape[0]
    combined_arrays = jnp.concatenate([thermal_anomaly, saltiness_anomaly, zonal_current, meridional_current, bottom_ocean_layer.astype(jnp.float32)[None]], axis=0)
    layer_count = combined_arrays.shape[0]
    fold_code = seam_axis_meridian[0]
    fold_type = jnp.mod(fold_code, 2).astype(jnp.int32)
    sign_column = jnp.concatenate([jnp.ones((2 * layer_number,), jnp.float32), -jnp.ones((2 * layer_number,), jnp.float32), jnp.ones((1,), jnp.float32)])[:, None, None]
    top_rows = combined_arrays[:, :, MERIDIAN_SPAN - 3:]
    mirror_cols = jnp.mod(fold_code - jnp.arange(PARALLEL_SPAN).astype(jnp.int32), PARALLEL_SPAN).astype(jnp.int32)
    source = jnp.take(top_rows, mirror_cols, axis=1)
    ghost = choose_rows(source, fold_type, sign_column)
    padded = jnp.concatenate([jnp.zeros((layer_count, PARALLEL_SPAN, 2), jnp.float32), combined_arrays, ghost], axis=2)
    grid_ext = jnp.concatenate([padded[:, PARALLEL_SPAN - 2:], padded, padded[:, :2]], axis=1)

    def band(band_index):
        first = (band_index * CY).astype(jnp.int32)
        piece = lax.dynamic_slice_in_dim(grid_ext, first, CY + 4, 2)
        mix_piece = lax.dynamic_slice_in_dim(interface_diffusivity, first, CY, 2)
        wind_piece = lax.dynamic_slice_in_dim(atmospheric_forcing, first, CY, 2)
        return advance(piece, mix_piece, wind_piece, first, MERIDIAN_SPAN)

    results = lax.map(band, jnp.arange(N_LAT).astype(jnp.int32))
    outputs = [jnp.transpose(item, (1, 2, 0, 3)).reshape(layer_number, PARALLEL_SPAN, MERIDIAN_SPAN) for item in results]
    return (outputs[0], outputs[1], outputs[2], outputs[3])
```

```python
import jax
import jax.numpy as jnp
from jax import lax
from jax.experimental import pallas as pl
from jax.experimental.pallas import tpu as pltpu
from jax.sharding import PartitionSpec as P

TIME_STEP = 0.2
TRACER_DIFF = 0.2
MOMENTUM_VISC = 0.2
THERMAL_EXPANSION = 0.5
HALINE_CONTRACTION = 0.4
WIND_GAIN = 2.0
VERTICAL_VISC = 1.0

K = 16
C = 8
R = 128

LANE_T, LANE_S, LANE_U, LANE_V, LANE_B = 0, 32, 64, 80, 96

LON_ROWS = 104
ROW_W, ROW_E = 0, LON_ROWS
ROW_S, ROW_N = 2 * LON_ROWS, 2 * LON_ROWS + 16
HALO_ROWS = 2 * LON_ROWS + 32


def pack_rows(fields, depth, pair, single):
    lane = lax.broadcasted_iota(jnp.int32, (C, R), 1)
    half = lane // 2
    out = jnp.zeros((C, R), jnp.float32)
    for field, first in zip(fields[:2], (LANE_T, LANE_S)):
        for k in range(K):
            at = first + 2 * k
            moved = pltpu.roll(field[k * C : (k + 1) * C, :], (at - pair) % R, 1)
            out = jnp.where(half == at // 2, moved, out)
    for field, first in zip(fields[2:], (LANE_U, LANE_V)):
        for k in range(K):
            at = first + k
            moved = pltpu.roll(field[k * C : (k + 1) * C, :], (at - single) % R, 1)
            out = jnp.where(lane == at, moved, out)
    moved = pltpu.roll(depth, (LANE_B - pair) % R, 1)
    return jnp.where(half == LANE_B // 2, moved, out)


def exchange_kernel(n_lon, n_lat, n_y, q_ref, t_ref, s_ref, u_ref, v_ref, b_ref, out_ref,
                    lon_out, lon_in, lat_out, lat_in, tiles, windows,
                    lon_sems, lat_sems, low_sems, high_sems):
    n_g = n_lon // n_y
    lon = lax.axis_index("lon")
    lat = lax.axis_index("lat")
    group = lon // n_y
    low = lon % n_y
    east = (lon + 1) % n_lon
    west = (lon + n_lon - 1) % n_lon
    is_top = lat == n_lat - 1
    has_north = lat < n_lat - 1
    has_south = lat > 0
    sides = (west, lon, east)

    def device(lon_at, lat_at):
        return {"lon": lon_at, "lat": lat_at}

    barrier = pltpu.get_barrier_semaphore()

    def greet(lon_at, lat_at):
        pl.semaphore_signal(barrier, inc=1, device_id=device(lon_at, lat_at),
                            device_id_type=pl.DeviceIdType.MESH)

    low_peers = [group * n_y + (low + d) % n_y for d in range(1, n_y)]
    high_peers = [((group + d) % n_g) * n_y + low for d in range(1, n_g)]

    @pl.when(is_top)
    def _():
        for peer in low_peers + high_peers:
            greet(peer, lat)

    greet(west, lat)
    greet(east, lat)

    @pl.when(has_north)
    def _():
        for side in sides:
            greet(side, lat + 1)

    @pl.when(has_south)
    def _():
        for side in sides:
            greet(side, lat - 1)

    fields = (t_ref, s_ref, u_ref, v_ref)
    depth = b_ref[...].astype(jnp.float32)

    def column(ref, at):
        return ref[pl.ds(at, K, stride=C), :]

    for slot, cols in ((0, (C - 2, C - 1)), (1, (0, 1))):
        near = cols[1] if slot == 0 else cols[0]
        lon_out[slot, 0:16, :] = column(t_ref, cols[0])
        lon_out[slot, 16:32, :] = column(t_ref, cols[1])
        lon_out[slot, 32:48, :] = column(s_ref, cols[0])
        lon_out[slot, 48:64, :] = column(s_ref, cols[1])
        lon_out[slot, 64:80, :] = column(u_ref, near)
        lon_out[slot, 80:96, :] = column(v_ref, near)
        rolled = depth if slot == 1 else pltpu.roll(depth, 2, 0)
        lon_out[slot, 96:104, :] = rolled

    upper = pack_rows(fields, depth, R - 2, R - 1)
    lat_out[0] = upper
    lat_out[1] = pack_rows(fields, depth, 0, 0)

    q = q_ref[0]

    @pl.when(is_top)
    def _():
        lower = pack_rows(fields, depth, R - 3, R - 2)
        chosen = jnp.where(q % 2 == 1, upper, lower)
        lane = lax.broadcasted_iota(jnp.int32, (C, R), 1)
        swapped = jnp.where(lane % 2 == 0, pltpu.roll(chosen, R - 1, 1), pltpu.roll(chosen, 1, 1))
        currents = jnp.logical_and(lane >= LANE_U, lane < LANE_B)
        tiles[pl.ds(pl.multiple_of(low * C, C), C), :] = jnp.where(currents, -chosen, swapped)

    lat_greets = jnp.where(has_north, 3, 0) + jnp.where(has_south, 3, 0)
    top_greets = jnp.where(is_top, n_y - 1 + n_g - 1, 0)
    pl.semaphore_wait(barrier, 2 + lat_greets + top_greets)

    def low_copy(d):
        mine = tiles.at[pl.ds(pl.multiple_of(low * C, C), C), :]
        return pltpu.make_async_remote_copy(
            src_ref=mine, dst_ref=mine, send_sem=low_sems.at[0, d - 1],
            recv_sem=low_sems.at[1, d - 1], device_id=device(low_peers[d - 1], lat),
            device_id_type=pl.DeviceIdType.MESH)

    def high_copy(d):
        mine = windows.at[pl.ds(pl.multiple_of(group * 16, 16), 16), :]
        return pltpu.make_async_remote_copy(
            src_ref=mine, dst_ref=mine, send_sem=high_sems.at[0, d - 1],
            recv_sem=high_sems.at[1, d - 1], device_id=device(high_peers[d - 1], lat),
            device_id_type=pl.DeviceIdType.MESH)

    @pl.when(is_top)
    def _():
        for d in range(1, n_y):
            low_copy(d).start()

    def lon_copy(slot):
        return pltpu.make_async_remote_copy(
            src_ref=lon_out.at[slot], dst_ref=lon_in.at[slot], send_sem=lon_sems.at[0, slot],
            recv_sem=lon_sems.at[1, slot], device_id=device((east, west)[slot], lat),
            device_id_type=pl.DeviceIdType.MESH)

    def lat_copy(direction, side):
        slot = 3 * direction + 2 - side
        return pltpu.make_async_remote_copy(
            src_ref=lat_out.at[direction], dst_ref=lat_in.at[slot],
            send_sem=lat_sems.at[0, slot], recv_sem=lat_sems.at[1, slot],
            device_id=device(sides[side], lat + 1 if direction == 0 else lat - 1),
            device_id_type=pl.DeviceIdType.MESH)

    @pl.when(has_north)
    def _():
        for side in range(3):
            lat_copy(0, side).start()

    @pl.when(has_south)
    def _():
        for side in range(3):
            lat_copy(1, side).start()

    for slot in range(2):
        lon_copy(slot).start()

    row = lax.broadcasted_iota(jnp.int32, (16, R), 0)

    def assemble(get):
        out = jnp.zeros((16, R), jnp.float32)
        for index in range(C + 2):
            out = jnp.where(row == index, get(index), out)
        return out

    @pl.when(is_top)
    def _():
        for d in range(1, n_y):
            low_copy(d).wait_recv()
        span = n_y * C

        def near(index):
            at = (q - C * low - (index - 1) + 4 * n_lon * C) % span
            return tiles[pl.ds(at, 1), :]

        windows[pl.ds(pl.multiple_of(group * 16, 16), 16), :] = assemble(near)
        for d in range(1, n_g):
            high_copy(d).start()

    for slot in range(2):
        lon_copy(slot).wait_recv()
    out_ref[ROW_W : ROW_W + LON_ROWS, :] = lon_in[0]
    out_ref[ROW_E : ROW_E + LON_ROWS, :] = lon_in[1]

    def side_rows(first):
        def get(index):
            if index == 0:
                return lat_in[first, C - 1 : C, :]
            if index == C + 1:
                return lat_in[first + 2, 0:1, :]
            return lat_in[first + 1, index - 1 : index, :]

        return assemble(get)

    @pl.when(has_south)
    def _():
        for side in range(3):
            lat_copy(0, 2 - side).wait_recv()
        out_ref[ROW_S : ROW_S + 16, :] = side_rows(0)

    @pl.when(jnp.logical_not(has_south))
    def _():
        out_ref[ROW_S : ROW_S + 16, :] = jnp.zeros((16, R), jnp.float32)

    @pl.when(has_north)
    def _():
        for side in range(3):
            lat_copy(1, 2 - side).wait_recv()
        out_ref[ROW_N : ROW_N + 16, :] = side_rows(3)

    @pl.when(is_top)
    def _():
        for d in range(1, n_g):
            high_copy(d).wait_recv()
        span = n_y * C

        def far(index):
            at = (q - C * lon - (index - 1) + 4 * n_lon * C) % (n_lon * C)
            return windows[pl.ds((at // span) * 16 + index, 1), :]

        out_ref[ROW_N : ROW_N + 16, :] = assemble(far)
        for d in range(1, n_y):
            low_copy(d).wait_send()
        for d in range(1, n_g):
            high_copy(d).wait_send()

    for slot in range(2):
        lon_copy(slot).wait_send()

    @pl.when(has_north)
    def _():
        for side in range(3):
            lat_copy(0, side).wait_send()

    @pl.when(has_south)
    def _():
        for side in range(3):
            lat_copy(1, side).wait_send()


def step_kernel(rows_total, t_ref, s_ref, u_ref, v_ref, b_ref, mix_ref, wind_ref, halo_ref,
                t_out, s_out, u_out, v_out, ratios):
    sub = lax.broadcasted_iota(jnp.int32, (C, R), 0)
    lane = lax.broadcasted_iota(jnp.int32, (C, R), 1)
    first_col, last_col = sub == 0, sub == C - 1
    first_row, last_row = lane == 0, lane == R - 1
    south_two, north_two = lane >= R - 2, lane < 2

    def halo(at):
        return jnp.broadcast_to(halo_ref[at : at + 1, :], (C, R))

    def west_of(x, edge):
        return jnp.where(first_col, edge, pltpu.roll(x, 1, 0))

    def east_of(x, edge):
        return jnp.where(last_col, edge, pltpu.roll(x, C - 1, 0))

    south = halo_ref[ROW_S + 1 : ROW_S + 1 + C, :]
    north = halo_ref[ROW_N + 1 : ROW_N + 1 + C, :]

    def south_of(x, at):
        return jnp.where(first_row, pltpu.roll(south, -at % R, 1), pltpu.roll(x, 1, 1))

    def north_of(x, at):
        return jnp.where(last_row, pltpu.roll(north, (R - 1 - at) % R, 1), pltpu.roll(x, R - 1, 1))

    def shifted_south(edge, corner, at):
        spread = lax.broadcasted_iota(jnp.int32, edge.shape, 1)
        return jnp.where(spread == 0, pltpu.roll(corner, -at % R, 1), pltpu.roll(edge, 1, 1))

    def shifted_north(edge, corner, at):
        spread = lax.broadcasted_iota(jnp.int32, edge.shape, 1)
        return jnp.where(spread == R - 1, pltpu.roll(corner, (R - 1 - at) % R, 1),
                         pltpu.roll(edge, R - 1, 1))

    north_west, north_east = halo(ROW_N), halo(ROW_N + C + 1)
    south_east = halo(ROW_S + C + 1)
    b = b_ref[...].astype(jnp.float32)
    bw_edge, be_edge, bee_edge = halo(ROW_W + 97), halo(ROW_E + 96), halo(ROW_E + 97)
    b_w = west_of(b, bw_edge)
    b_e = east_of(b, be_edge)
    b_ee = east_of(b_e, bee_edge)
    b_s = south_of(b, LANE_B + 1)
    b_n = north_of(b, LANE_B)
    b_nn = north_of(b_n, LANE_B + 1)
    b_nw = west_of(b_n, shifted_north(bw_edge, north_west, LANE_B))
    b_ne = east_of(b_n, shifted_north(be_edge, north_east, LANE_B))
    b_se = east_of(b_s, shifted_south(be_edge, south_east, LANE_B + 1))
    least = jnp.minimum
    d_u, d_v = least(b, b_e), least(b, b_n)
    d_uw, d_vs = least(b, b_w), least(b, b_s)
    u_pairs = (least(d_u, b_ee), least(d_uw, d_u), least(d_u, least(b_n, b_ne)),
               least(d_u, least(b_s, b_se)))
    v_pairs = (least(d_v, least(b_e, b_ne)), least(d_v, least(b_w, b_nw)), least(d_v, b_nn),
               least(d_v, d_vs))

    base = (lax.axis_index("lat") * R + lane).astype(jnp.float32)
    cor_u = 2.0 * (base + 0.5) / rows_total - 1.0
    cor_v = 2.0 * (base + 1.0) / rows_total - 1.0

    zero = jnp.zeros((C, R), jnp.float32)
    sum_x, sum_y = zero, zero
    above = [zero, zero, zero]
    ratio = [zero, zero, zero]
    value = [zero] * 4
    outs = (t_out, s_out, u_out, v_out)
    kinds = (0, 0, 1, 2)

    for k in range(K):
        def keep(depth, x):
            return jnp.where(depth > k, x, 0.0)

        u = u_ref[k]
        v = v_ref[k]
        uw_edge = halo(ROW_W + 64 + k)
        vw_edge = halo(ROW_W + 80 + k)
        ue_edge = halo(ROW_E + 64 + k)
        ve_edge = halo(ROW_E + 80 + k)
        u_w = west_of(u, uw_edge)
        u_e = east_of(u, ue_edge)
        u_s = south_of(u, LANE_U + k)
        u_n = north_of(u, LANE_U + k)
        v_w = west_of(v, vw_edge)
        v_e = east_of(v, ve_edge)
        v_s = south_of(v, LANE_V + k)
        v_n = north_of(v, LANE_V + k)

        fx = keep(d_u, u) * (1.0 / 12.0)
        fx_w = keep(d_uw, u_w) * (1.0 / 12.0)
        fy = keep(d_v, v) * (1.0 / 12.0)
        fy_s = keep(d_vs, v_s) * (1.0 / 12.0)

        stars, easts, norths, centres = [], [], [], []
        for ref, block, first in ((t_ref, 0, LANE_T), (s_ref, 32, LANE_S)):
            c = ref[k]
            c_w = west_of(c, halo(ROW_W + block + 16 + k))
            c_ww = west_of(c_w, halo(ROW_W + block + k))
            c_e = east_of(c, halo(ROW_E + block + k))
            c_ee = east_of(c_e, halo(ROW_E + block + 16 + k))
            at = first + 2 * k
            below = pltpu.roll(south, (R - 2 - at) % R, 1)
            c_s = pltpu.roll(jnp.where(last_row, below, c), 1, 1)
            c_ss = pltpu.roll(jnp.where(south_two, below, c), 2, 1)
            beyond = pltpu.roll(north, -at % R, 1)
            c_n = pltpu.roll(jnp.where(first_row, beyond, c), R - 1, 1)
            c_nn = pltpu.roll(jnp.where(north_two, beyond, c), R - 2, 1)
            advect = (
                fx_w * (7.0 * (c_w + c) - (c_ww + c_e)) - fx * (7.0 * (c + c_e) - (c_w + c_ee))
            ) + (
                fy_s * (7.0 * (c_s + c) - (c_ss + c_n)) - fy * (7.0 * (c + c_n) - (c_s + c_nn))
            )
            spread = (keep(b_e, c_e - c) + keep(b_w, c_w - c)) + (
                keep(b_n, c_n - c) + keep(b_s, c_s - c))
            stars.append(c + keep(b, TIME_STEP * (advect + TRACER_DIFF * spread)))
            centres.append(c)
            easts.append(c_e)
            norths.append(c_n)

        def buoyancy(depth, pair):
            return keep(depth, THERMAL_EXPANSION * pair[0] - HALINE_CONTRACTION * pair[1])

        here = buoyancy(b, centres)
        step_x = buoyancy(b_e, easts) - here
        step_y = buoyancy(b_n, norths) - here
        sum_x = sum_x + step_x
        sum_y = sum_y + step_y

        pair_v = v + v_s
        edge_v = ve_edge + shifted_south(ve_edge, south_east, LANE_V + k)
        v_at_u = 0.25 * (pair_v + east_of(pair_v, edge_v))
        pair_u = u + u_n
        edge_u = uw_edge + shifted_north(uw_edge, north_west, LANE_U + k)
        u_at_v = 0.25 * (pair_u + west_of(pair_u, edge_u))
        u_visc = (keep(u_pairs[0], u_e - u) + keep(u_pairs[1], u_w - u)) + (
            keep(u_pairs[2], u_n - u) + keep(u_pairs[3], u_s - u))
        v_visc = (keep(v_pairs[0], v_e - v) + keep(v_pairs[1], v_w - v)) + (
            keep(v_pairs[2], v_n - v) + keep(v_pairs[3], v_s - v))
        u_star = u + TIME_STEP * (
            cor_u * v_at_u - (sum_x - 0.5 * step_x) + MOMENTUM_VISC * u_visc)
        v_star = v + TIME_STEP * (
            -cor_v * u_at_v - (sum_y - 0.5 * step_y) + MOMENTUM_VISC * v_visc)
        if k == 0:
            u_star = u_star + TIME_STEP * WIND_GAIN * wind_ref[0]
            v_star = v_star + TIME_STEP * WIND_GAIN * wind_ref[1]
        stars.append(keep(d_u, u_star))
        stars.append(keep(d_v, v_star))

        inverse = []
        nexts = []
        for kind, depth in enumerate((b, d_u, d_v)):
            if k == K - 1:
                coupling = zero
            elif kind == 0:
                coupling = jnp.where(depth > k + 1, TIME_STEP * mix_ref[k], 0.0)
            else:
                coupling = jnp.where(depth > k + 1, TIME_STEP * VERTICAL_VISC, 0.0)
            denom = 1.0 + coupling + above[kind] * (1.0 + ratio[kind])
            inv = 1.0 / denom
            inverse.append(inv)
            nexts.append(coupling)
        for index in range(4):
            kind = kinds[index]
            value[index] = (stars[index] + above[kind] * value[index]) * inverse[kind]
            outs[index][k] = value[index]
        for kind in range(3):
            above[kind] = nexts[kind]
            ratio[kind] = -nexts[kind] * inverse[kind]
            ratios[kind, k] = ratio[kind]

    result = list(value)
    for k in range(K - 2, -1, -1):
        for index in range(4):
            result[index] = outs[index][k] - ratios[kinds[index], k] * result[index]
            outs[index][k] = result[index]


def shards(thermal_anomaly, saltiness_anomaly, zonal_current, meridional_current,
           bottom_ocean_layer, seam_axis_meridian, interface_diffusivity, atmospheric_forcing):
    n_lon = lax.axis_size("lon")
    n_lat = lax.axis_size("lat")
    n_y = 8 if n_lon >= 64 else n_lon // 2
    n_g = n_lon // n_y
    fields = (thermal_anomaly, saltiness_anomaly, zonal_current, meridional_current)
    vmem = pl.BlockSpec(memory_space=pltpu.VMEM)
    f32 = jnp.float32

    def exchange_body(*refs):
        exchange_kernel(n_lon, n_lat, n_y, *refs)

    def step_body(*refs):
        step_kernel(R * n_lat, *refs)

    halo = pl.pallas_call(
        exchange_body,
        name="exchange",
        out_shape=jax.ShapeDtypeStruct((HALO_ROWS, R), f32),
        in_specs=[pl.BlockSpec(memory_space=pltpu.SMEM)] + [vmem] * 5,
        out_specs=vmem,
        scratch_shapes=[
            pltpu.VMEM((2, LON_ROWS, R), f32),
            pltpu.VMEM((2, LON_ROWS, R), f32),
            pltpu.VMEM((2, C, R), f32),
            pltpu.VMEM((6, C, R), f32),
            pltpu.VMEM((n_y * C, R), f32),
            pltpu.VMEM((n_g * 16, R), f32),
            pltpu.SemaphoreType.DMA((2, 2)),
            pltpu.SemaphoreType.DMA((2, 6)),
            pltpu.SemaphoreType.DMA((2, n_y - 1)),
            pltpu.SemaphoreType.DMA((2, n_g - 1)),
        ],
        compiler_params=pltpu.CompilerParams(collective_id=0, has_side_effects=True),
    )(seam_axis_meridian, *[field.reshape(K * C, R) for field in fields], bottom_ocean_layer)
    return pl.pallas_call(
        step_body,
        name="step",
        out_shape=tuple(jax.ShapeDtypeStruct((K, C, R), f32) for _ in range(4)),
        in_specs=[vmem] * 8,
        out_specs=(vmem,) * 4,
        scratch_shapes=[pltpu.VMEM((3, K, C, R), f32)],
    )(*fields, bottom_ocean_layer, interface_diffusivity, atmospheric_forcing, halo)


def solution(mesh):
    grid = P(None, "lon", "lat")
    return jax.shard_map(
        shards,
        mesh=mesh,
        in_specs=(grid, grid, grid, grid, P("lon", "lat"), P(), grid, grid),
        out_specs=(grid,) * 4,
        check_vma=False,
    )
```

```python
import jax
import jax.numpy as jnp
from jax import lax
from jax.experimental import pallas as pl
from jax.experimental.pallas import tpu as pltpu
from jax.sharding import PartitionSpec as P

TIME_STEP = 0.2
TRACER_DIFF = 0.2
MOMENTUM_VISC = 0.2
THERMAL_EXPANSION = 0.5
HALINE_CONTRACTION = 0.4
WIND_GAIN = 2.0
VERTICAL_VISC = 1.0

K = 16
C = 8
R = 128

LANE_T, LANE_S, LANE_U, LANE_V, LANE_B = 0, 32, 64, 80, 96

LON_ROWS = 104
ROW_W, ROW_E = 0, LON_ROWS
ROW_S, ROW_N = 2 * LON_ROWS, 2 * LON_ROWS + 16
HALO_ROWS = 2 * LON_ROWS + 32


def pack_rows(fields, depth, pair, single):
    lane = lax.broadcasted_iota(jnp.int32, (C, R), 1)
    half = lane // 2
    out = jnp.zeros((C, R), jnp.float32)
    for field, first in zip(fields[:2], (LANE_T, LANE_S)):
        for k in range(K):
            at = first + 2 * k
            moved = pltpu.roll(field[k * C : (k + 1) * C, :], (at - pair) % R, 1)
            out = jnp.where(half == at // 2, moved, out)
    for field, first in zip(fields[2:], (LANE_U, LANE_V)):
        for k in range(K):
            at = first + k
            moved = pltpu.roll(field[k * C : (k + 1) * C, :], (at - single) % R, 1)
            out = jnp.where(lane == at, moved, out)
    moved = pltpu.roll(depth, (LANE_B - pair) % R, 1)
    return jnp.where(half == LANE_B // 2, moved, out)


def exchange_kernel(n_lon, n_lat, n_y, q_any, t_any, s_any, u_any, v_any, b_any, out_ref,
                    q_ref, t_ref, s_ref, u_ref, v_ref, b_ref,
                    lon_out, lon_in, lat_out, lat_in, tiles, windows,
                    load_sems, lon_sems, lat_sems, low_sems, high_sems):
    n_g = n_lon // n_y
    lon = lax.axis_index("lon")
    lat = lax.axis_index("lat")
    group = lon // n_y
    low = lon % n_y
    east = (lon + 1) % n_lon
    west = (lon + n_lon - 1) % n_lon
    is_top = lat == n_lat - 1
    has_north = lat < n_lat - 1
    has_south = lat > 0
    sides = (west, lon, east)

    def device(lon_at, lat_at):
        return {"lon": lon_at, "lat": lat_at}

    barrier = pltpu.get_barrier_semaphore()

    def greet(lon_at, lat_at):
        pl.semaphore_signal(barrier, inc=1, device_id=device(lon_at, lat_at),
                            device_id_type=pl.DeviceIdType.MESH)

    low_peers = [group * n_y + (low + d) % n_y for d in range(1, n_y)]
    high_peers = [((group + d) % n_g) * n_y + low for d in range(1, n_g)]

    @pl.when(is_top)
    def _():
        for peer in low_peers + high_peers:
            greet(peer, lat)

    loads = [
        pltpu.make_async_copy(source, target, load_sems.at[at])
        for at, (source, target) in enumerate(
            zip((q_any, t_any, s_any, u_any, v_any, b_any),
                (q_ref, t_ref, s_ref, u_ref, v_ref, b_ref)))
    ]
    for load in loads:
        load.start()

    greet(west, lat)
    greet(east, lat)

    @pl.when(has_north)
    def _():
        for side in sides:
            greet(side, lat + 1)

    @pl.when(has_south)
    def _():
        for side in sides:
            greet(side, lat - 1)

    for load in loads:
        load.wait()
    fields = (t_ref, s_ref, u_ref, v_ref)
    depth = b_ref[...].astype(jnp.float32)

    def column(ref, at):
        return ref[pl.ds(at, K, stride=C), :]

    def pack_columns():
        for slot, cols in ((0, (C - 2, C - 1)), (1, (0, 1))):
            near = cols[1] if slot == 0 else cols[0]
            lon_out[slot, 0:16, :] = column(t_ref, cols[0])
            lon_out[slot, 16:32, :] = column(t_ref, cols[1])
            lon_out[slot, 32:48, :] = column(s_ref, cols[0])
            lon_out[slot, 48:64, :] = column(s_ref, cols[1])
            lon_out[slot, 64:80, :] = column(u_ref, near)
            lon_out[slot, 80:96, :] = column(v_ref, near)
            rolled = depth if slot == 1 else pltpu.roll(depth, 2, 0)
            lon_out[slot, 96:104, :] = rolled

    def pack_south():
        lat_out[1] = pack_rows(fields, depth, 0, 0)

    upper = pack_rows(fields, depth, R - 2, R - 1)
    lat_out[0] = upper
    q = q_ref[0]

    @pl.when(is_top)
    def _():
        lower = pack_rows(fields, depth, R - 3, R - 2)
        chosen = jnp.where((q & 1) == 1, upper, lower)
        lane = lax.broadcasted_iota(jnp.int32, (C, R), 1)
        swapped = jnp.where(lane % 2 == 0, pltpu.roll(chosen, R - 1, 1), pltpu.roll(chosen, 1, 1))
        currents = jnp.logical_and(lane >= LANE_U, lane < LANE_B)
        tiles[pl.ds(pl.multiple_of(low * C, C), C), :] = jnp.where(currents, -chosen, swapped)

    @pl.when(jnp.logical_not(is_top))
    def _():
        pack_south()
        pack_columns()

    lat_greets = jnp.where(has_north, 3, 0) + jnp.where(has_south, 3, 0)
    top_greets = jnp.where(is_top, n_y - 1 + n_g - 1, 0)
    pl.semaphore_wait(barrier, 2 + lat_greets + top_greets)

    def low_copy(d):
        mine = tiles.at[pl.ds(pl.multiple_of(low * C, C), C), :]
        return pltpu.make_async_remote_copy(
            src_ref=mine, dst_ref=mine, send_sem=low_sems.at[0, d - 1],
            recv_sem=low_sems.at[1, d - 1], device_id=device(low_peers[d - 1], lat),
            device_id_type=pl.DeviceIdType.MESH)

    def high_copy(d):
        mine = windows.at[pl.ds(pl.multiple_of(group * 16, 16), 16), :]
        return pltpu.make_async_remote_copy(
            src_ref=mine, dst_ref=mine, send_sem=high_sems.at[0, d - 1],
            recv_sem=high_sems.at[1, d - 1], device_id=device(high_peers[d - 1], lat),
            device_id_type=pl.DeviceIdType.MESH)

    @pl.when(is_top)
    def _():
        for d in range(1, n_y):
            low_copy(d).start()
        pack_south()

    def lon_copy(slot):
        return pltpu.make_async_remote_copy(
            src_ref=lon_out.at[slot], dst_ref=lon_in.at[slot], send_sem=lon_sems.at[0, slot],
            recv_sem=lon_sems.at[1, slot], device_id=device((east, west)[slot], lat),
            device_id_type=pl.DeviceIdType.MESH)

    def lat_copy(direction, side):
        slot = 3 * direction + 2 - side
        return pltpu.make_async_remote_copy(
            src_ref=lat_out.at[direction], dst_ref=lat_in.at[slot],
            send_sem=lat_sems.at[0, slot], recv_sem=lat_sems.at[1, slot],
            device_id=device(sides[side], lat + 1 if direction == 0 else lat - 1),
            device_id_type=pl.DeviceIdType.MESH)

    @pl.when(has_north)
    def _():
        for side in range(3):
            lat_copy(0, side).start()

    @pl.when(has_south)
    def _():
        for side in range(3):
            lat_copy(1, side).start()

    @pl.when(jnp.logical_not(is_top))
    def _():
        for slot in range(2):
            lon_copy(slot).start()

    row = lax.broadcasted_iota(jnp.int32, (16, R), 0)

    def assemble(get):
        out = jnp.zeros((16, R), jnp.float32)
        for index in range(C + 2):
            out = jnp.where(row == index, get(index), out)
        return out

    @pl.when(is_top)
    def _():
        pack_columns()
        for d in range(1, n_y):
            low_copy(d).wait_recv()
        span = n_y * C

        def near(index):
            at = (q - C * low - (index - 1) + 4 * n_lon * C) & (span - 1)
            return tiles[pl.ds(at, 1), :]

        windows[pl.ds(pl.multiple_of(group * 16, 16), 16), :] = assemble(near)
        for d in range(1, n_g):
            high_copy(d).start()
        for slot in range(2):
            lon_copy(slot).start()

    for slot in range(2):
        lon_copy(slot).wait_recv()
    out_ref[ROW_W : ROW_W + LON_ROWS, :] = lon_in[0]
    out_ref[ROW_E : ROW_E + LON_ROWS, :] = lon_in[1]

    def side_rows(first):
        def get(index):
            if index == 0:
                return lat_in[first, C - 1 : C, :]
            if index == C + 1:
                return lat_in[first + 2, 0:1, :]
            return lat_in[first + 1, index - 1 : index, :]

        return assemble(get)

    @pl.when(has_south)
    def _():
        for side in range(3):
            lat_copy(0, 2 - side).wait_recv()
        out_ref[ROW_S : ROW_S + 16, :] = side_rows(0)

    @pl.when(jnp.logical_not(has_south))
    def _():
        out_ref[ROW_S : ROW_S + 16, :] = jnp.zeros((16, R), jnp.float32)

    @pl.when(has_north)
    def _():
        for side in range(3):
            lat_copy(1, 2 - side).wait_recv()
        out_ref[ROW_N : ROW_N + 16, :] = side_rows(3)

    @pl.when(is_top)
    def _():
        for d in range(1, n_g):
            high_copy(d).wait_recv()
        span = n_y * C

        def far(index):
            at = (q - C * lon - (index - 1) + 4 * n_lon * C) & (n_lon * C - 1)
            return windows[pl.ds(lax.shift_right_logical(at, span.bit_length() - 1) * 16 + index, 1), :]

        out_ref[ROW_N : ROW_N + 16, :] = assemble(far)
        for d in range(1, n_y):
            low_copy(d).wait_send()
        for d in range(1, n_g):
            high_copy(d).wait_send()

    for slot in range(2):
        lon_copy(slot).wait_send()

    @pl.when(has_north)
    def _():
        for side in range(3):
            lat_copy(0, side).wait_send()

    @pl.when(has_south)
    def _():
        for side in range(3):
            lat_copy(1, side).wait_send()


def step_kernel(rows_total, t_ref, s_ref, u_ref, v_ref, b_ref, mix_ref, wind_ref, halo_ref,
                t_out, s_out, u_out, v_out, ratios):
    sub = lax.broadcasted_iota(jnp.int32, (C, R), 0)
    lane = lax.broadcasted_iota(jnp.int32, (C, R), 1)
    first_col, last_col = sub == 0, sub == C - 1
    first_row, last_row = lane == 0, lane == R - 1
    south_two, north_two = lane >= R - 2, lane < 2

    def halo(at):
        return jnp.broadcast_to(halo_ref[at : at + 1, :], (C, R))

    def west_of(x, edge):
        return jnp.where(first_col, edge, pltpu.roll(x, 1, 0))

    def east_of(x, edge):
        return jnp.where(last_col, edge, pltpu.roll(x, C - 1, 0))

    south = halo_ref[ROW_S + 1 : ROW_S + 1 + C, :]
    north = halo_ref[ROW_N + 1 : ROW_N + 1 + C, :]

    def south_of(x, at):
        return jnp.where(first_row, pltpu.roll(south, -at % R, 1), pltpu.roll(x, 1, 1))

    def north_of(x, at):
        return jnp.where(last_row, pltpu.roll(north, (R - 1 - at) % R, 1), pltpu.roll(x, R - 1, 1))

    def shifted_south(edge, corner, at):
        spread = lax.broadcasted_iota(jnp.int32, edge.shape, 1)
        return jnp.where(spread == 0, pltpu.roll(corner, -at % R, 1), pltpu.roll(edge, 1, 1))

    def shifted_north(edge, corner, at):
        spread = lax.broadcasted_iota(jnp.int32, edge.shape, 1)
        return jnp.where(spread == R - 1, pltpu.roll(corner, (R - 1 - at) % R, 1),
                         pltpu.roll(edge, R - 1, 1))

    north_west, north_east = halo(ROW_N), halo(ROW_N + C + 1)
    south_east = halo(ROW_S + C + 1)
    b = b_ref[...].astype(jnp.float32)
    bw_edge, be_edge, bee_edge = halo(ROW_W + 97), halo(ROW_E + 96), halo(ROW_E + 97)
    b_w = west_of(b, bw_edge)
    b_e = east_of(b, be_edge)
    b_ee = east_of(b_e, bee_edge)
    b_s = south_of(b, LANE_B + 1)
    b_n = north_of(b, LANE_B)
    b_nn = north_of(b_n, LANE_B + 1)
    b_nw = west_of(b_n, shifted_north(bw_edge, north_west, LANE_B))
    b_ne = east_of(b_n, shifted_north(be_edge, north_east, LANE_B))
    b_se = east_of(b_s, shifted_south(be_edge, south_east, LANE_B + 1))
    least = jnp.minimum
    d_u, d_v = least(b, b_e), least(b, b_n)
    d_uw, d_vs = least(b, b_w), least(b, b_s)
    u_pairs = (least(d_u, b_ee), least(d_uw, d_u), least(d_u, least(b_n, b_ne)),
               least(d_u, least(b_s, b_se)))
    v_pairs = (least(d_v, least(b_e, b_ne)), least(d_v, least(b_w, b_nw)), least(d_v, b_nn),
               least(d_v, d_vs))

    base = (lax.axis_index("lat") * R + lane).astype(jnp.float32)
    cor_u = 2.0 * (base + 0.5) / rows_total - 1.0
    cor_v = 2.0 * (base + 1.0) / rows_total - 1.0

    zero = jnp.zeros((C, R), jnp.float32)
    sum_x, sum_y = zero, zero
    above = [zero, zero, zero]
    ratio = [zero, zero, zero]
    value = [zero] * 4
    outs = (t_out, s_out, u_out, v_out)
    kinds = (0, 0, 1, 2)

    for k in range(K):
        def keep(depth, x):
            return jnp.where(depth > k, x, 0.0)

        u = u_ref[k]
        v = v_ref[k]
        uw_edge = halo(ROW_W + 64 + k)
        vw_edge = halo(ROW_W + 80 + k)
        ue_edge = halo(ROW_E + 64 + k)
        ve_edge = halo(ROW_E + 80 + k)
        u_w = west_of(u, uw_edge)
        u_e = east_of(u, ue_edge)
        u_s = south_of(u, LANE_U + k)
        u_n = north_of(u, LANE_U + k)
        v_w = west_of(v, vw_edge)
        v_e = east_of(v, ve_edge)
        v_s = south_of(v, LANE_V + k)
        v_n = north_of(v, LANE_V + k)

        fx = keep(d_u, u) * (1.0 / 12.0)
        fx_w = keep(d_uw, u_w) * (1.0 / 12.0)
        fy = keep(d_v, v) * (1.0 / 12.0)
        fy_s = keep(d_vs, v_s) * (1.0 / 12.0)

        stars, easts, norths, centres = [], [], [], []
        for ref, block, first in ((t_ref, 0, LANE_T), (s_ref, 32, LANE_S)):
            c = ref[k]
            c_w = west_of(c, halo(ROW_W + block + 16 + k))
            c_ww = west_of(c_w, halo(ROW_W + block + k))
            c_e = east_of(c, halo(ROW_E + block + k))
            c_ee = east_of(c_e, halo(ROW_E + block + 16 + k))
            at = first + 2 * k
            below = pltpu.roll(south, (R - 2 - at) % R, 1)
            c_s = pltpu.roll(jnp.where(last_row, below, c), 1, 1)
            c_ss = pltpu.roll(jnp.where(south_two, below, c), 2, 1)
            beyond = pltpu.roll(north, -at % R, 1)
            c_n = pltpu.roll(jnp.where(first_row, beyond, c), R - 1, 1)
            c_nn = pltpu.roll(jnp.where(north_two, beyond, c), R - 2, 1)
            advect = (
                fx_w * (7.0 * (c_w + c) - (c_ww + c_e)) - fx * (7.0 * (c + c_e) - (c_w + c_ee))
            ) + (
                fy_s * (7.0 * (c_s + c) - (c_ss + c_n)) - fy * (7.0 * (c + c_n) - (c_s + c_nn))
            )
            spread = (keep(b_e, c_e - c) + keep(b_w, c_w - c)) + (
                keep(b_n, c_n - c) + keep(b_s, c_s - c))
            stars.append(c + keep(b, TIME_STEP * (advect + TRACER_DIFF * spread)))
            centres.append(c)
            easts.append(c_e)
            norths.append(c_n)

        def buoyancy(depth, pair):
            return keep(depth, THERMAL_EXPANSION * pair[0] - HALINE_CONTRACTION * pair[1])

        here = buoyancy(b, centres)
        step_x = buoyancy(b_e, easts) - here
        step_y = buoyancy(b_n, norths) - here
        sum_x = sum_x + step_x
        sum_y = sum_y + step_y

        pair_v = v + v_s
        edge_v = ve_edge + shifted_south(ve_edge, south_east, LANE_V + k)
        v_at_u = 0.25 * (pair_v + east_of(pair_v, edge_v))
        pair_u = u + u_n
        edge_u = uw_edge + shifted_north(uw_edge, north_west, LANE_U + k)
        u_at_v = 0.25 * (pair_u + west_of(pair_u, edge_u))
        u_visc = (keep(u_pairs[0], u_e - u) + keep(u_pairs[1], u_w - u)) + (
            keep(u_pairs[2], u_n - u) + keep(u_pairs[3], u_s - u))
        v_visc = (keep(v_pairs[0], v_e - v) + keep(v_pairs[1], v_w - v)) + (
            keep(v_pairs[2], v_n - v) + keep(v_pairs[3], v_s - v))
        u_star = u + TIME_STEP * (
            cor_u * v_at_u - (sum_x - 0.5 * step_x) + MOMENTUM_VISC * u_visc)
        v_star = v + TIME_STEP * (
            -cor_v * u_at_v - (sum_y - 0.5 * step_y) + MOMENTUM_VISC * v_visc)
        if k == 0:
            u_star = u_star + TIME_STEP * WIND_GAIN * wind_ref[0]
            v_star = v_star + TIME_STEP * WIND_GAIN * wind_ref[1]
        stars.append(keep(d_u, u_star))
        stars.append(keep(d_v, v_star))

        inverse = []
        nexts = []
        for kind, depth in enumerate((b, d_u, d_v)):
            if k == K - 1:
                coupling = zero
            elif kind == 0:
                coupling = jnp.where(depth > k + 1, TIME_STEP * mix_ref[k], 0.0)
            else:
                coupling = jnp.where(depth > k + 1, TIME_STEP * VERTICAL_VISC, 0.0)
            denom = 1.0 + coupling + above[kind] * (1.0 + ratio[kind])
            inv = 1.0 / denom
            inverse.append(inv)
            nexts.append(coupling)
        for index in range(4):
            kind = kinds[index]
            value[index] = (stars[index] + above[kind] * value[index]) * inverse[kind]
            outs[index][k] = value[index]
        for kind in range(3):
            above[kind] = nexts[kind]
            ratio[kind] = -nexts[kind] * inverse[kind]
            ratios[kind, k] = ratio[kind]

    result = list(value)
    for k in range(K - 2, -1, -1):
        for index in range(4):
            result[index] = outs[index][k] - ratios[kinds[index], k] * result[index]
            outs[index][k] = result[index]


def shards(thermal_anomaly, saltiness_anomaly, zonal_current, meridional_current,
           bottom_ocean_layer, seam_axis_meridian, interface_diffusivity, atmospheric_forcing):
    n_lon = lax.axis_size("lon")
    n_lat = lax.axis_size("lat")
    n_y = 8 if n_lon >= 64 else n_lon // 2
    n_g = n_lon // n_y
    fields = (thermal_anomaly, saltiness_anomaly, zonal_current, meridional_current)
    vmem = pl.BlockSpec(memory_space=pltpu.VMEM)
    f32 = jnp.float32

    def exchange_body(*refs):
        exchange_kernel(n_lon, n_lat, n_y, *refs)

    def step_body(*refs):
        step_kernel(R * n_lat, *refs)

    halo = pl.pallas_call(
        exchange_body,
        name="exchange",
        out_shape=jax.ShapeDtypeStruct((HALO_ROWS, R), f32),
        in_specs=[pl.BlockSpec(memory_space=pltpu.HBM)] * 6,
        out_specs=vmem,
        scratch_shapes=[
            pltpu.SMEM((1,), jnp.int32),
            *[pltpu.VMEM((K * C, R), f32) for _ in range(4)],
            pltpu.VMEM((C, R), jnp.int32),
            pltpu.VMEM((2, LON_ROWS, R), f32),
            pltpu.VMEM((2, LON_ROWS, R), f32),
            pltpu.VMEM((2, C, R), f32),
            pltpu.VMEM((6, C, R), f32),
            pltpu.VMEM((n_y * C, R), f32),
            pltpu.VMEM((n_g * 16, R), f32),
            pltpu.SemaphoreType.DMA((6,)),
            pltpu.SemaphoreType.DMA((2, 2)),
            pltpu.SemaphoreType.DMA((2, 6)),
            pltpu.SemaphoreType.DMA((2, n_y - 1)),
            pltpu.SemaphoreType.DMA((2, n_g - 1)),
        ],
        compiler_params=pltpu.CompilerParams(collective_id=0, has_side_effects=True,
                                             vmem_limit_bytes=4 << 20),
    )(seam_axis_meridian, *[
        pltpu.with_memory_space_constraint(operand, pltpu.HBM)
        for operand in (*[field.reshape(K * C, R) for field in fields], bottom_ocean_layer)
    ])
    return pl.pallas_call(
        step_body,
        name="step",
        out_shape=tuple(jax.ShapeDtypeStruct((K, C, R), f32) for _ in range(4)),
        in_specs=[vmem] * 8,
        out_specs=(vmem,) * 4,
        scratch_shapes=[pltpu.VMEM((3, K, C, R), f32)],
        compiler_params=pltpu.CompilerParams(vmem_limit_bytes=4 << 20),
    )(*fields, bottom_ocean_layer, interface_diffusivity, atmospheric_forcing, halo)


def solution(mesh):
    grid = P(None, "lon", "lat")
    return jax.shard_map(
        shards,
        mesh=mesh,
        in_specs=(grid, grid, grid, grid, P("lon", "lat"), P(), grid, grid),
        out_specs=(grid,) * 4,
        check_vma=False,
    )
```

```python
import jax
import jax.numpy as jnp
from jax import lax
from jax.experimental import pallas as pl
from jax.experimental.pallas import tpu as pltpu
from jax.sharding import PartitionSpec as P

TIME_STEP = 0.2
TRACER_DIFF = 0.2
MOMENTUM_VISC = 0.2
THERMAL_EXPANSION = 0.5
HALINE_CONTRACTION = 0.4
WIND_GAIN = 2.0
VERTICAL_VISC = 1.0

K = 16
C = 8
R = 128

LANE_T, LANE_S, LANE_U, LANE_V, LANE_B = 0, 32, 64, 80, 96

LON_ROWS = 104
ROW_W, ROW_E = 0, LON_ROWS
ROW_S, ROW_N = 2 * LON_ROWS, 2 * LON_ROWS + 16
HALO_ROWS = 2 * LON_ROWS + 32


def pack_rows(fields, depth, pair, single):
    lane = lax.broadcasted_iota(jnp.int32, (C, R), 1)
    half = lane // 2
    out = jnp.zeros((C, R), jnp.float32)
    for field, first in zip(fields[:2], (LANE_T, LANE_S)):
        for k in range(K):
            at = first + 2 * k
            moved = pltpu.roll(field[k * C : (k + 1) * C, :], (at - pair) % R, 1)
            out = jnp.where(half == at // 2, moved, out)
    for field, first in zip(fields[2:], (LANE_U, LANE_V)):
        for k in range(K):
            at = first + k
            moved = pltpu.roll(field[k * C : (k + 1) * C, :], (at - single) % R, 1)
            out = jnp.where(lane == at, moved, out)
    moved = pltpu.roll(depth, (LANE_B - pair) % R, 1)
    return jnp.where(half == LANE_B // 2, moved, out)


PART_T, PART_S, PART_P, PART_U, PART_INV, PART_RATIO, PARTS = 0, 1, 2, 3, 4, 5, 6


def east_west(t_ref, s_ref, u_ref, b, mix_ref, halo_ref, part_ref):
    sub = lax.broadcasted_iota(jnp.int32, (C, R), 0)
    first_col, last_col = sub == 0, sub == C - 1

    def halo(at):
        return jnp.broadcast_to(halo_ref[at : at + 1, :], (C, R))

    def west_of(x, edge):
        return jnp.where(first_col, edge, pltpu.roll(x, 1, 0))

    def east_of(x, edge):
        return jnp.where(last_col, edge, pltpu.roll(x, C - 1, 0))

    b_w = west_of(b, halo(ROW_W + 97))
    b_e = east_of(b, halo(ROW_E + 96))
    b_ee = east_of(b_e, halo(ROW_E + 97))
    d_u, d_uw = jnp.minimum(b, b_e), jnp.minimum(b, b_w)
    d_ue, d_uww = jnp.minimum(d_u, b_ee), jnp.minimum(d_uw, d_u)
    zero = jnp.zeros((C, R), jnp.float32)
    total, above, ratio = zero, zero, zero
    for k in range(K):
        def keep(depth, x):
            return jnp.where(depth > k, x, 0.0)

        def level(ref):
            return ref[k * C : (k + 1) * C, :]

        u = level(u_ref)
        u_w = west_of(u, halo(ROW_W + 64 + k))
        u_e = east_of(u, halo(ROW_E + 64 + k))
        fx = keep(d_u, u) * (1.0 / 12.0)
        fx_w = keep(d_uw, u_w) * (1.0 / 12.0)
        here, there = [], []
        for part, ref, block in ((PART_T, t_ref, 0), (PART_S, s_ref, 32)):
            c = level(ref)
            c_w = west_of(c, halo(ROW_W + block + 16 + k))
            c_ww = west_of(c_w, halo(ROW_W + block + k))
            c_e = east_of(c, halo(ROW_E + block + k))
            c_ee = east_of(c_e, halo(ROW_E + block + 16 + k))
            advect = (
                fx_w * (7.0 * (c_w + c) - (c_ww + c_e)) - fx * (7.0 * (c + c_e) - (c_w + c_ee))
            )
            part_ref[part, k] = advect + TRACER_DIFF * (keep(b_e, c_e - c) + keep(b_w, c_w - c))
            here.append(c)
            there.append(c_e)

        def buoyancy(depth, pair):
            return keep(depth, THERMAL_EXPANSION * pair[0] - HALINE_CONTRACTION * pair[1])

        change = buoyancy(b_e, there) - buoyancy(b, here)
        total = total + change
        part_ref[PART_P, k] = total - 0.5 * change
        part_ref[PART_U, k] = keep(d_ue, u_e - u) + keep(d_uww, u_w - u)
        coupling = zero if k == K - 1 else jnp.where(b > k + 1, TIME_STEP * mix_ref[k], 0.0)
        inv = 1.0 / (1.0 + coupling + above * (1.0 + ratio))
        above, ratio = coupling, -coupling * inv
        part_ref[PART_INV, k] = inv
        part_ref[PART_RATIO, k] = ratio


def exchange_kernel(n_lon, n_lat, n_y, q_any, t_any, s_any, u_any, v_any, b_any, mix_any,
                    out_ref, part_ref, q_ref, t_ref, s_ref, u_ref, v_ref, b_ref, mix_ref,
                    lon_out, lon_in, lat_out, lat_in, tiles, windows,
                    load_sems, lon_sems, lat_sems, low_sems, high_sems):
    n_g = n_lon // n_y
    lon = lax.axis_index("lon")
    lat = lax.axis_index("lat")
    group = lon // n_y
    low = lon % n_y
    east = (lon + 1) % n_lon
    west = (lon + n_lon - 1) % n_lon
    is_top = lat == n_lat - 1
    has_north = lat < n_lat - 1
    has_south = lat > 0
    sides = (west, lon, east)

    def device(lon_at, lat_at):
        return {"lon": lon_at, "lat": lat_at}

    barrier = pltpu.get_barrier_semaphore()

    def greet(lon_at, lat_at):
        pl.semaphore_signal(barrier, inc=1, device_id=device(lon_at, lat_at),
                            device_id_type=pl.DeviceIdType.MESH)

    low_peers = [group * n_y + (low + d) % n_y for d in range(1, n_y)]
    high_peers = [((group + d) % n_g) * n_y + low for d in range(1, n_g)]

    @pl.when(is_top)
    def _():
        for peer in low_peers + high_peers:
            greet(peer, lat)

    loads = [
        pltpu.make_async_copy(source, target, load_sems.at[at])
        for at, (source, target) in enumerate(
            zip((q_any, t_any, s_any, u_any, v_any, b_any),
                (q_ref, t_ref, s_ref, u_ref, v_ref, b_ref)))
    ]
    for load in loads:
        load.start()
    mix_load = pltpu.make_async_copy(mix_any, mix_ref, load_sems.at[6])
    mix_load.start()

    greet(west, lat)
    greet(east, lat)

    @pl.when(has_north)
    def _():
        for side in sides:
            greet(side, lat + 1)

    @pl.when(has_south)
    def _():
        for side in sides:
            greet(side, lat - 1)

    for load in loads:
        load.wait()
    fields = (t_ref, s_ref, u_ref, v_ref)
    depth = b_ref[...].astype(jnp.float32)

    def column(ref, at):
        return ref[pl.ds(at, K, stride=C), :]

    def pack_columns():
        for slot, cols in ((0, (C - 2, C - 1)), (1, (0, 1))):
            near = cols[1] if slot == 0 else cols[0]
            lon_out[slot, 0:16, :] = column(t_ref, cols[0])
            lon_out[slot, 16:32, :] = column(t_ref, cols[1])
            lon_out[slot, 32:48, :] = column(s_ref, cols[0])
            lon_out[slot, 48:64, :] = column(s_ref, cols[1])
            lon_out[slot, 64:80, :] = column(u_ref, near)
            lon_out[slot, 80:96, :] = column(v_ref, near)
            rolled = depth if slot == 1 else pltpu.roll(depth, 2, 0)
            lon_out[slot, 96:104, :] = rolled

    def pack_south():
        lat_out[1] = pack_rows(fields, depth, 0, 0)

    upper = pack_rows(fields, depth, R - 2, R - 1)
    lat_out[0] = upper
    q = q_ref[0]

    @pl.when(is_top)
    def _():
        lower = pack_rows(fields, depth, R - 3, R - 2)
        chosen = jnp.where((q & 1) == 1, upper, lower)
        lane = lax.broadcasted_iota(jnp.int32, (C, R), 1)
        swapped = jnp.where(lane % 2 == 0, pltpu.roll(chosen, R - 1, 1), pltpu.roll(chosen, 1, 1))
        currents = jnp.logical_and(lane >= LANE_U, lane < LANE_B)
        tiles[pl.ds(pl.multiple_of(low * C, C), C), :] = jnp.where(currents, -chosen, swapped)

    @pl.when(jnp.logical_not(is_top))
    def _():
        pack_south()
        pack_columns()

    lat_greets = jnp.where(has_north, 3, 0) + jnp.where(has_south, 3, 0)
    top_greets = jnp.where(is_top, n_y - 1 + n_g - 1, 0)
    pl.semaphore_wait(barrier, 2 + lat_greets + top_greets)

    def low_copy(d):
        mine = tiles.at[pl.ds(pl.multiple_of(low * C, C), C), :]
        return pltpu.make_async_remote_copy(
            src_ref=mine, dst_ref=mine, send_sem=low_sems.at[0, d - 1],
            recv_sem=low_sems.at[1, d - 1], device_id=device(low_peers[d - 1], lat),
            device_id_type=pl.DeviceIdType.MESH)

    def high_copy(d):
        mine = windows.at[pl.ds(pl.multiple_of(group * 16, 16), 16), :]
        return pltpu.make_async_remote_copy(
            src_ref=mine, dst_ref=mine, send_sem=high_sems.at[0, d - 1],
            recv_sem=high_sems.at[1, d - 1], device_id=device(high_peers[d - 1], lat),
            device_id_type=pl.DeviceIdType.MESH)

    @pl.when(is_top)
    def _():
        for d in range(1, n_y):
            low_copy(d).start()
        pack_south()

    def lon_copy(slot):
        return pltpu.make_async_remote_copy(
            src_ref=lon_out.at[slot], dst_ref=lon_in.at[slot], send_sem=lon_sems.at[0, slot],
            recv_sem=lon_sems.at[1, slot], device_id=device((east, west)[slot], lat),
            device_id_type=pl.DeviceIdType.MESH)

    def lat_copy(direction, side):
        slot = 3 * direction + 2 - side
        return pltpu.make_async_remote_copy(
            src_ref=lat_out.at[direction], dst_ref=lat_in.at[slot],
            send_sem=lat_sems.at[0, slot], recv_sem=lat_sems.at[1, slot],
            device_id=device(sides[side], lat + 1 if direction == 0 else lat - 1),
            device_id_type=pl.DeviceIdType.MESH)

    @pl.when(has_north)
    def _():
        for side in range(3):
            lat_copy(0, side).start()

    @pl.when(has_south)
    def _():
        for side in range(3):
            lat_copy(1, side).start()

    @pl.when(jnp.logical_not(is_top))
    def _():
        for slot in range(2):
            lon_copy(slot).start()

    row = lax.broadcasted_iota(jnp.int32, (16, R), 0)

    def assemble(get):
        out = jnp.zeros((16, R), jnp.float32)
        for index in range(C + 2):
            out = jnp.where(row == index, get(index), out)
        return out

    @pl.when(is_top)
    def _():
        pack_columns()
        for d in range(1, n_y):
            low_copy(d).wait_recv()
        span = n_y * C

        def near(index):
            at = (q - C * low - (index - 1) + 4 * n_lon * C) & (span - 1)
            return tiles[pl.ds(at, 1), :]

        windows[pl.ds(pl.multiple_of(group * 16, 16), 16), :] = assemble(near)
        for d in range(1, n_g):
            high_copy(d).start()
        for slot in range(2):
            lon_copy(slot).start()

    for slot in range(2):
        lon_copy(slot).wait_recv()
    out_ref[ROW_W : ROW_W + LON_ROWS, :] = lon_in[0]
    out_ref[ROW_E : ROW_E + LON_ROWS, :] = lon_in[1]
    mix_load.wait()
    east_west(t_ref, s_ref, u_ref, depth, mix_ref, out_ref, part_ref)

    def side_rows(first):
        def get(index):
            if index == 0:
                return lat_in[first, C - 1 : C, :]
            if index == C + 1:
                return lat_in[first + 2, 0:1, :]
            return lat_in[first + 1, index - 1 : index, :]

        return assemble(get)

    @pl.when(has_south)
    def _():
        for side in range(3):
            lat_copy(0, 2 - side).wait_recv()
        out_ref[ROW_S : ROW_S + 16, :] = side_rows(0)

    @pl.when(jnp.logical_not(has_south))
    def _():
        out_ref[ROW_S : ROW_S + 16, :] = jnp.zeros((16, R), jnp.float32)

    @pl.when(has_north)
    def _():
        for side in range(3):
            lat_copy(1, 2 - side).wait_recv()
        out_ref[ROW_N : ROW_N + 16, :] = side_rows(3)

    @pl.when(is_top)
    def _():
        for d in range(1, n_g):
            high_copy(d).wait_recv()
        span = n_y * C

        def far(index):
            at = (q - C * lon - (index - 1) + 4 * n_lon * C) & (n_lon * C - 1)
            return windows[pl.ds(lax.shift_right_logical(at, span.bit_length() - 1) * 16 + index, 1), :]

        out_ref[ROW_N : ROW_N + 16, :] = assemble(far)
        for d in range(1, n_y):
            low_copy(d).wait_send()
        for d in range(1, n_g):
            high_copy(d).wait_send()

    for slot in range(2):
        lon_copy(slot).wait_send()

    @pl.when(has_north)
    def _():
        for side in range(3):
            lat_copy(0, side).wait_send()

    @pl.when(has_south)
    def _():
        for side in range(3):
            lat_copy(1, side).wait_send()


def step_kernel(rows_total, t_ref, s_ref, u_ref, v_ref, b_ref, mix_ref, wind_ref, halo_ref, part_ref,
                t_out, s_out, u_out, v_out, ratios):
    sub = lax.broadcasted_iota(jnp.int32, (C, R), 0)
    lane = lax.broadcasted_iota(jnp.int32, (C, R), 1)
    first_col, last_col = sub == 0, sub == C - 1
    first_row, last_row = lane == 0, lane == R - 1
    south_two, north_two = lane >= R - 2, lane < 2

    def halo(at):
        return jnp.broadcast_to(halo_ref[at : at + 1, :], (C, R))

    def west_of(x, edge):
        return jnp.where(first_col, edge, pltpu.roll(x, 1, 0))

    def east_of(x, edge):
        return jnp.where(last_col, edge, pltpu.roll(x, C - 1, 0))

    south = halo_ref[ROW_S + 1 : ROW_S + 1 + C, :]
    north = halo_ref[ROW_N + 1 : ROW_N + 1 + C, :]

    def south_of(x, at):
        return jnp.where(first_row, pltpu.roll(south, -at % R, 1), pltpu.roll(x, 1, 1))

    def north_of(x, at):
        return jnp.where(last_row, pltpu.roll(north, (R - 1 - at) % R, 1), pltpu.roll(x, R - 1, 1))

    def shifted_south(edge, corner, at):
        spread = lax.broadcasted_iota(jnp.int32, edge.shape, 1)
        return jnp.where(spread == 0, pltpu.roll(corner, -at % R, 1), pltpu.roll(edge, 1, 1))

    def shifted_north(edge, corner, at):
        spread = lax.broadcasted_iota(jnp.int32, edge.shape, 1)
        return jnp.where(spread == R - 1, pltpu.roll(corner, (R - 1 - at) % R, 1),
                         pltpu.roll(edge, R - 1, 1))

    north_west, north_east = halo(ROW_N), halo(ROW_N + C + 1)
    south_east = halo(ROW_S + C + 1)
    b = b_ref[...].astype(jnp.float32)
    bw_edge, be_edge = halo(ROW_W + 97), halo(ROW_E + 96)
    b_w = west_of(b, bw_edge)
    b_e = east_of(b, be_edge)
    b_s = south_of(b, LANE_B + 1)
    b_n = north_of(b, LANE_B)
    b_nn = north_of(b_n, LANE_B + 1)
    b_nw = west_of(b_n, shifted_north(bw_edge, north_west, LANE_B))
    b_ne = east_of(b_n, shifted_north(be_edge, north_east, LANE_B))
    b_se = east_of(b_s, shifted_south(be_edge, south_east, LANE_B + 1))
    least = jnp.minimum
    d_u, d_v = least(b, b_e), least(b, b_n)
    d_vs = least(b, b_s)
    d_un, d_us = least(d_u, least(b_n, b_ne)), least(d_u, least(b_s, b_se))
    v_pairs = (least(d_v, least(b_e, b_ne)), least(d_v, least(b_w, b_nw)), least(d_v, b_nn),
               least(d_v, d_vs))

    base = (lax.axis_index("lat") * R + lane).astype(jnp.float32)
    cor_u = 2.0 * (base + 0.5) / rows_total - 1.0
    cor_v = 2.0 * (base + 1.0) / rows_total - 1.0

    zero = jnp.zeros((C, R), jnp.float32)
    sum_y = zero
    above = [zero, zero, zero]
    ratio = [zero, zero, zero]
    value = [zero] * 4
    outs = (t_out, s_out, u_out, v_out)
    kinds = (0, 0, 1, 2)

    for k in range(K):
        def keep(depth, x):
            return jnp.where(depth > k, x, 0.0)

        u = u_ref[k]
        v = v_ref[k]
        uw_edge = halo(ROW_W + 64 + k)
        vw_edge = halo(ROW_W + 80 + k)
        ve_edge = halo(ROW_E + 80 + k)
        u_s = south_of(u, LANE_U + k)
        u_n = north_of(u, LANE_U + k)
        v_w = west_of(v, vw_edge)
        v_e = east_of(v, ve_edge)
        v_s = south_of(v, LANE_V + k)
        v_n = north_of(v, LANE_V + k)

        fy = keep(d_v, v) * (1.0 / 12.0)
        fy_s = keep(d_vs, v_s) * (1.0 / 12.0)

        stars, norths, centres = [], [], []
        for part, ref, first in ((PART_T, t_ref, LANE_T), (PART_S, s_ref, LANE_S)):
            c = ref[k]
            at = first + 2 * k
            below = pltpu.roll(south, (R - 2 - at) % R, 1)
            c_s = pltpu.roll(jnp.where(last_row, below, c), 1, 1)
            c_ss = pltpu.roll(jnp.where(south_two, below, c), 2, 1)
            beyond = pltpu.roll(north, -at % R, 1)
            c_n = pltpu.roll(jnp.where(first_row, beyond, c), R - 1, 1)
            c_nn = pltpu.roll(jnp.where(north_two, beyond, c), R - 2, 1)
            advect = (
                fy_s * (7.0 * (c_s + c) - (c_ss + c_n)) - fy * (7.0 * (c + c_n) - (c_s + c_nn))
            )
            spread = keep(b_n, c_n - c) + keep(b_s, c_s - c)
            stars.append(c + keep(b, TIME_STEP * (part_ref[part, k] + (advect + TRACER_DIFF * spread))))
            centres.append(c)
            norths.append(c_n)

        def buoyancy(depth, pair):
            return keep(depth, THERMAL_EXPANSION * pair[0] - HALINE_CONTRACTION * pair[1])

        here = buoyancy(b, centres)
        step_y = buoyancy(b_n, norths) - here
        sum_y = sum_y + step_y

        pair_v = v + v_s
        edge_v = ve_edge + shifted_south(ve_edge, south_east, LANE_V + k)
        v_at_u = 0.25 * (pair_v + east_of(pair_v, edge_v))
        pair_u = u + u_n
        edge_u = uw_edge + shifted_north(uw_edge, north_west, LANE_U + k)
        u_at_v = 0.25 * (pair_u + west_of(pair_u, edge_u))
        u_visc = part_ref[PART_U, k] + (keep(d_un, u_n - u) + keep(d_us, u_s - u))
        v_visc = (keep(v_pairs[0], v_e - v) + keep(v_pairs[1], v_w - v)) + (
            keep(v_pairs[2], v_n - v) + keep(v_pairs[3], v_s - v))
        u_star = u + TIME_STEP * (
            cor_u * v_at_u - part_ref[PART_P, k] + MOMENTUM_VISC * u_visc)
        v_star = v + TIME_STEP * (
            -cor_v * u_at_v - (sum_y - 0.5 * step_y) + MOMENTUM_VISC * v_visc)
        if k == 0:
            u_star = u_star + TIME_STEP * WIND_GAIN * wind_ref[0]
            v_star = v_star + TIME_STEP * WIND_GAIN * wind_ref[1]
        stars.append(keep(d_u, u_star))
        stars.append(keep(d_v, v_star))

        inverse = []
        nexts = []
        for kind, depth in enumerate((b, d_u, d_v)):
            if k == K - 1:
                coupling = zero
            elif kind == 0:
                coupling = jnp.where(depth > k + 1, TIME_STEP * mix_ref[k], 0.0)
            else:
                coupling = jnp.where(depth > k + 1, TIME_STEP * VERTICAL_VISC, 0.0)
            if kind == 0:
                inv = part_ref[PART_INV, k]
            else:
                inv = 1.0 / (1.0 + coupling + above[kind] * (1.0 + ratio[kind]))
            inverse.append(inv)
            nexts.append(coupling)
        for index in range(4):
            kind = kinds[index]
            value[index] = (stars[index] + above[kind] * value[index]) * inverse[kind]
            outs[index][k] = value[index]
        above[0] = nexts[0]
        for kind in (1, 2):
            above[kind] = nexts[kind]
            ratio[kind] = -nexts[kind] * inverse[kind]
            ratios[kind - 1, k] = ratio[kind]

    result = list(value)
    for k in range(K - 2, -1, -1):
        for index in range(4):
            kind = kinds[index]
            factor = part_ref[PART_RATIO, k] if kind == 0 else ratios[kind - 1, k]
            result[index] = outs[index][k] - factor * result[index]
            outs[index][k] = result[index]


def shards(thermal_anomaly, saltiness_anomaly, zonal_current, meridional_current,
           bottom_ocean_layer, seam_axis_meridian, interface_diffusivity, atmospheric_forcing):
    n_lon = lax.axis_size("lon")
    n_lat = lax.axis_size("lat")
    n_y = 8 if n_lon >= 64 else n_lon // 2
    n_g = n_lon // n_y
    fields = (thermal_anomaly, saltiness_anomaly, zonal_current, meridional_current)
    vmem = pl.BlockSpec(memory_space=pltpu.VMEM)
    f32 = jnp.float32

    def exchange_body(*refs):
        exchange_kernel(n_lon, n_lat, n_y, *refs)

    def step_body(*refs):
        step_kernel(R * n_lat, *refs)

    halo, part = pl.pallas_call(
        exchange_body,
        name="exchange",
        out_shape=(jax.ShapeDtypeStruct((HALO_ROWS, R), f32),
                   jax.ShapeDtypeStruct((PARTS, K, C, R), f32)),
        in_specs=[pl.BlockSpec(memory_space=pltpu.HBM)] * 7,
        out_specs=(vmem, vmem),
        scratch_shapes=[
            pltpu.SMEM((1,), jnp.int32),
            *[pltpu.VMEM((K * C, R), f32) for _ in range(4)],
            pltpu.VMEM((C, R), jnp.int32),
            pltpu.VMEM((K - 1, C, R), f32),
            pltpu.VMEM((2, LON_ROWS, R), f32),
            pltpu.VMEM((2, LON_ROWS, R), f32),
            pltpu.VMEM((2, C, R), f32),
            pltpu.VMEM((6, C, R), f32),
            pltpu.VMEM((n_y * C, R), f32),
            pltpu.VMEM((n_g * 16, R), f32),
            pltpu.SemaphoreType.DMA((7,)),
            pltpu.SemaphoreType.DMA((2, 2)),
            pltpu.SemaphoreType.DMA((2, 6)),
            pltpu.SemaphoreType.DMA((2, n_y - 1)),
            pltpu.SemaphoreType.DMA((2, n_g - 1)),
        ],
        compiler_params=pltpu.CompilerParams(collective_id=0, has_side_effects=True,
                                             vmem_limit_bytes=4 << 20),
    )(seam_axis_meridian, *[
        pltpu.with_memory_space_constraint(operand, pltpu.HBM)
        for operand in (*[field.reshape(K * C, R) for field in fields], bottom_ocean_layer,
                        interface_diffusivity)
    ])
    return pl.pallas_call(
        step_body,
        name="step",
        out_shape=tuple(jax.ShapeDtypeStruct((K, C, R), f32) for _ in range(4)),
        in_specs=[vmem] * 9,
        out_specs=(vmem,) * 4,
        scratch_shapes=[pltpu.VMEM((2, K, C, R), f32)],
        compiler_params=pltpu.CompilerParams(vmem_limit_bytes=4 << 20),
    )(*fields, bottom_ocean_layer, interface_diffusivity, atmospheric_forcing, halo,
      part)


def solution(mesh):
    grid = P(None, "lon", "lat")
    return jax.shard_map(
        shards,
        mesh=mesh,
        in_specs=(grid, grid, grid, grid, P("lon", "lat"), P(), grid, grid),
        out_specs=(grid,) * 4,
        check_vma=False,
    )
```

```python
import jax
import jax.numpy as jnp
from jax import lax
from jax.experimental import pallas as pl
from jax.experimental.pallas import tpu as pltpu
from jax.sharding import PartitionSpec as P

TIME_STEP = 0.2
TRACER_DIFF = 0.2
MOMENTUM_VISC = 0.2
THERMAL_EXPANSION = 0.5
HALINE_CONTRACTION = 0.4
WIND_GAIN = 2.0
VERTICAL_VISC = 1.0

K = 16
C = 8
R = 128

LANE_T, LANE_S, LANE_U, LANE_V, LANE_B = 0, 32, 64, 80, 96

LON_ROWS = 104
ROW_W, ROW_E = 0, LON_ROWS
ROW_S, ROW_N = 2 * LON_ROWS, 2 * LON_ROWS + 16
HALO_ROWS = 2 * LON_ROWS + 32


DRAG = TIME_STEP * VERTICAL_VISC
INNER, LAST = [], []
for _k in range(K):
    _above = DRAG * (1.0 - DRAG * INNER[-1]) if _k else 0.0
    INNER.append(1.0 / (1.0 + _above + DRAG))
    LAST.append(1.0 / (1.0 + _above))


def pack_rows(fields, depth, pair, single):
    lane = lax.broadcasted_iota(jnp.int32, (C, R), 1)
    half = lane // 2
    out = jnp.zeros((C, R), jnp.float32)
    for field, first in zip(fields[:2], (LANE_T, LANE_S)):
        for k in range(K):
            at = first + 2 * k
            moved = pltpu.roll(field[k * C : (k + 1) * C, :], (at - pair) % R, 1)
            out = jnp.where(half == at // 2, moved, out)
    for field, first in zip(fields[2:], (LANE_U, LANE_V)):
        for k in range(K):
            at = first + k
            moved = pltpu.roll(field[k * C : (k + 1) * C, :], (at - single) % R, 1)
            out = jnp.where(lane == at, moved, out)
    moved = pltpu.roll(depth, (LANE_B - pair) % R, 1)
    return jnp.where(half == LANE_B // 2, moved, out)


PART_T, PART_S, PART_P, PART_U, PART_INV, PART_RATIO, PARTS = 0, 1, 2, 3, 4, 5, 6


def east_west(t_ref, s_ref, u_ref, b, mix_ref, halo_ref, part_ref):
    sub = lax.broadcasted_iota(jnp.int32, (C, R), 0)
    first_col, last_col = sub == 0, sub == C - 1

    def halo(at):
        return jnp.broadcast_to(halo_ref[at : at + 1, :], (C, R))

    def west_of(x, edge):
        return jnp.where(first_col, edge, pltpu.roll(x, 1, 0))

    def east_of(x, edge):
        return jnp.where(last_col, edge, pltpu.roll(x, C - 1, 0))

    b_w = west_of(b, halo(ROW_W + 97))
    b_e = east_of(b, halo(ROW_E + 96))
    b_ee = east_of(b_e, halo(ROW_E + 97))
    d_u, d_uw = jnp.minimum(b, b_e), jnp.minimum(b, b_w)
    d_ue, d_uww = jnp.minimum(d_u, b_ee), jnp.minimum(d_uw, d_u)
    zero = jnp.zeros((C, R), jnp.float32)
    total, above, ratio = zero, zero, zero
    for k in range(K):
        def keep(depth, x):
            return jnp.where(depth > k, x, 0.0)

        def level(ref):
            return ref[k * C : (k + 1) * C, :]

        u = level(u_ref)
        u_w = west_of(u, halo(ROW_W + 64 + k))
        u_e = east_of(u, halo(ROW_E + 64 + k))
        fx = keep(d_u, u) * (1.0 / 12.0)
        fx_w = keep(d_uw, u_w) * (1.0 / 12.0)
        here, there = [], []
        for part, ref, block in ((PART_T, t_ref, 0), (PART_S, s_ref, 32)):
            c = level(ref)
            c_w = west_of(c, halo(ROW_W + block + 16 + k))
            c_ww = west_of(c_w, halo(ROW_W + block + k))
            c_e = east_of(c, halo(ROW_E + block + k))
            c_ee = east_of(c_e, halo(ROW_E + block + 16 + k))
            advect = (
                fx_w * (7.0 * (c_w + c) - (c_ww + c_e)) - fx * (7.0 * (c + c_e) - (c_w + c_ee))
            )
            part_ref[part, k] = advect + TRACER_DIFF * (keep(b_e, c_e - c) + keep(b_w, c_w - c))
            here.append(c)
            there.append(c_e)

        def buoyancy(depth, pair):
            return keep(depth, THERMAL_EXPANSION * pair[0] - HALINE_CONTRACTION * pair[1])

        change = buoyancy(b_e, there) - buoyancy(b, here)
        total = total + change
        part_ref[PART_P, k] = total - 0.5 * change
        part_ref[PART_U, k] = keep(d_ue, u_e - u) + keep(d_uww, u_w - u)
        coupling = zero if k == K - 1 else jnp.where(b > k + 1, TIME_STEP * mix_ref[k], 0.0)
        inv = 1.0 / (1.0 + coupling + above * (1.0 + ratio))
        above, ratio = coupling, -coupling * inv
        part_ref[PART_INV, k] = inv
        part_ref[PART_RATIO, k] = ratio


def exchange_kernel(n_lon, n_lat, n_y, q_any, t_any, s_any, u_any, v_any, b_any, mix_any,
                    out_ref, part_ref, q_ref, t_ref, s_ref, u_ref, v_ref, b_ref, mix_ref,
                    lon_out, lon_in, lat_out, lat_in, tiles, windows,
                    load_sems, lon_sems, lat_sems, low_sems, high_sems):
    n_g = n_lon // n_y
    lon = lax.axis_index("lon")
    lat = lax.axis_index("lat")
    group = lon // n_y
    low = lon % n_y
    east = (lon + 1) % n_lon
    west = (lon + n_lon - 1) % n_lon
    is_top = lat == n_lat - 1
    has_north = lat < n_lat - 1
    has_south = lat > 0
    sides = (west, lon, east)

    def device(lon_at, lat_at):
        return {"lon": lon_at, "lat": lat_at}

    barrier = pltpu.get_barrier_semaphore()

    def greet(lon_at, lat_at):
        pl.semaphore_signal(barrier, inc=1, device_id=device(lon_at, lat_at),
                            device_id_type=pl.DeviceIdType.MESH)

    low_peers = [group * n_y + (low + d) % n_y for d in range(1, n_y)]
    high_peers = [((group + d) % n_g) * n_y + low for d in range(1, n_g)]

    @pl.when(is_top)
    def _():
        for peer in low_peers + high_peers:
            greet(peer, lat)

    loads = [
        pltpu.make_async_copy(source, target, load_sems.at[at])
        for at, (source, target) in enumerate(
            zip((q_any, t_any, s_any, u_any, v_any, b_any),
                (q_ref, t_ref, s_ref, u_ref, v_ref, b_ref)))
    ]
    for load in loads:
        load.start()
    mix_load = pltpu.make_async_copy(mix_any, mix_ref, load_sems.at[6])
    mix_load.start()

    greet(west, lat)
    greet(east, lat)

    @pl.when(has_north)
    def _():
        for side in sides:
            greet(side, lat + 1)

    @pl.when(has_south)
    def _():
        for side in sides:
            greet(side, lat - 1)

    for load in loads:
        load.wait()
    fields = (t_ref, s_ref, u_ref, v_ref)
    depth = b_ref[...].astype(jnp.float32)

    def column(ref, at):
        return ref[pl.ds(at, K, stride=C), :]

    def pack_columns():
        for slot, cols in ((0, (C - 2, C - 1)), (1, (0, 1))):
            near = cols[1] if slot == 0 else cols[0]
            lon_out[slot, 0:16, :] = column(t_ref, cols[0])
            lon_out[slot, 16:32, :] = column(t_ref, cols[1])
            lon_out[slot, 32:48, :] = column(s_ref, cols[0])
            lon_out[slot, 48:64, :] = column(s_ref, cols[1])
            lon_out[slot, 64:80, :] = column(u_ref, near)
            lon_out[slot, 80:96, :] = column(v_ref, near)
            rolled = depth if slot == 1 else pltpu.roll(depth, 2, 0)
            lon_out[slot, 96:104, :] = rolled

    def pack_south():
        lat_out[1] = pack_rows(fields, depth, 0, 0)

    upper = pack_rows(fields, depth, R - 2, R - 1)
    lat_out[0] = upper
    q = q_ref[0]

    @pl.when(is_top)
    def _():
        lower = pack_rows(fields, depth, R - 3, R - 2)
        chosen = jnp.where((q & 1) == 1, upper, lower)
        lane = lax.broadcasted_iota(jnp.int32, (C, R), 1)
        swapped = jnp.where(lane % 2 == 0, pltpu.roll(chosen, R - 1, 1), pltpu.roll(chosen, 1, 1))
        currents = jnp.logical_and(lane >= LANE_U, lane < LANE_B)
        tiles[pl.ds(pl.multiple_of(low * C, C), C), :] = jnp.where(currents, -chosen, swapped)

    @pl.when(jnp.logical_not(is_top))
    def _():
        pack_south()
        pack_columns()

    lat_greets = jnp.where(has_north, 3, 0) + jnp.where(has_south, 3, 0)
    top_greets = jnp.where(is_top, n_y - 1 + n_g - 1, 0)
    pl.semaphore_wait(barrier, 2 + lat_greets + top_greets)

    def low_copy(d):
        mine = tiles.at[pl.ds(pl.multiple_of(low * C, C), C), :]
        return pltpu.make_async_remote_copy(
            src_ref=mine, dst_ref=mine, send_sem=low_sems.at[0, d - 1],
            recv_sem=low_sems.at[1, d - 1], device_id=device(low_peers[d - 1], lat),
            device_id_type=pl.DeviceIdType.MESH)

    def high_copy(d):
        mine = windows.at[pl.ds(pl.multiple_of(group * 16, 16), 16), :]
        return pltpu.make_async_remote_copy(
            src_ref=mine, dst_ref=mine, send_sem=high_sems.at[0, d - 1],
            recv_sem=high_sems.at[1, d - 1], device_id=device(high_peers[d - 1], lat),
            device_id_type=pl.DeviceIdType.MESH)

    @pl.when(is_top)
    def _():
        for d in range(1, n_y):
            low_copy(d).start()
        pack_south()

    def lon_copy(slot):
        return pltpu.make_async_remote_copy(
            src_ref=lon_out.at[slot], dst_ref=lon_in.at[slot], send_sem=lon_sems.at[0, slot],
            recv_sem=lon_sems.at[1, slot], device_id=device((east, west)[slot], lat),
            device_id_type=pl.DeviceIdType.MESH)

    def lat_copy(direction, side):
        slot = 3 * direction + 2 - side
        return pltpu.make_async_remote_copy(
            src_ref=lat_out.at[direction], dst_ref=lat_in.at[slot],
            send_sem=lat_sems.at[0, slot], recv_sem=lat_sems.at[1, slot],
            device_id=device(sides[side], lat + 1 if direction == 0 else lat - 1),
            device_id_type=pl.DeviceIdType.MESH)

    @pl.when(has_north)
    def _():
        for side in range(3):
            lat_copy(0, side).start()

    @pl.when(has_south)
    def _():
        for side in range(3):
            lat_copy(1, side).start()

    @pl.when(jnp.logical_not(is_top))
    def _():
        for slot in range(2):
            lon_copy(slot).start()

    row = lax.broadcasted_iota(jnp.int32, (16, R), 0)

    def assemble(get):
        out = jnp.zeros((16, R), jnp.float32)
        for index in range(C + 2):
            out = jnp.where(row == index, get(index), out)
        return out

    @pl.when(is_top)
    def _():
        pack_columns()
        for d in range(1, n_y):
            low_copy(d).wait_recv()
        span = n_y * C

        def near(index):
            at = (q - C * low - (index - 1) + 4 * n_lon * C) & (span - 1)
            return tiles[pl.ds(at, 1), :]

        windows[pl.ds(pl.multiple_of(group * 16, 16), 16), :] = assemble(near)
        for d in range(1, n_g):
            high_copy(d).start()
        for slot in range(2):
            lon_copy(slot).start()

    for slot in range(2):
        lon_copy(slot).wait_recv()
    out_ref[ROW_W : ROW_W + LON_ROWS, :] = lon_in[0]
    out_ref[ROW_E : ROW_E + LON_ROWS, :] = lon_in[1]
    mix_load.wait()
    east_west(t_ref, s_ref, u_ref, depth, mix_ref, out_ref, part_ref)

    def side_rows(first):
        def get(index):
            if index == 0:
                return lat_in[first, C - 1 : C, :]
            if index == C + 1:
                return lat_in[first + 2, 0:1, :]
            return lat_in[first + 1, index - 1 : index, :]

        return assemble(get)

    @pl.when(has_south)
    def _():
        for side in range(3):
            lat_copy(0, 2 - side).wait_recv()
        out_ref[ROW_S : ROW_S + 16, :] = side_rows(0)

    @pl.when(jnp.logical_not(has_south))
    def _():
        out_ref[ROW_S : ROW_S + 16, :] = jnp.zeros((16, R), jnp.float32)

    @pl.when(has_north)
    def _():
        for side in range(3):
            lat_copy(1, 2 - side).wait_recv()
        out_ref[ROW_N : ROW_N + 16, :] = side_rows(3)

    @pl.when(is_top)
    def _():
        for d in range(1, n_g):
            high_copy(d).wait_recv()
        span = n_y * C

        def far(index):
            at = (q - C * lon - (index - 1) + 4 * n_lon * C) & (n_lon * C - 1)
            return windows[pl.ds(lax.shift_right_logical(at, span.bit_length() - 1) * 16 + index, 1), :]

        out_ref[ROW_N : ROW_N + 16, :] = assemble(far)
        for d in range(1, n_y):
            low_copy(d).wait_send()
        for d in range(1, n_g):
            high_copy(d).wait_send()

    for slot in range(2):
        lon_copy(slot).wait_send()

    @pl.when(has_north)
    def _():
        for side in range(3):
            lat_copy(0, side).wait_send()

    @pl.when(has_south)
    def _():
        for side in range(3):
            lat_copy(1, side).wait_send()


def step_kernel(rows_total, t_ref, s_ref, u_ref, v_ref, b_ref, mix_ref, wind_ref, halo_ref, part_ref,
                t_out, s_out, u_out, v_out):
    sub = lax.broadcasted_iota(jnp.int32, (C, R), 0)
    lane = lax.broadcasted_iota(jnp.int32, (C, R), 1)
    first_col, last_col = sub == 0, sub == C - 1
    first_row, last_row = lane == 0, lane == R - 1
    south_two, north_two = lane >= R - 2, lane < 2

    def halo(at):
        return jnp.broadcast_to(halo_ref[at : at + 1, :], (C, R))

    def west_of(x, edge):
        return jnp.where(first_col, edge, pltpu.roll(x, 1, 0))

    def east_of(x, edge):
        return jnp.where(last_col, edge, pltpu.roll(x, C - 1, 0))

    south = halo_ref[ROW_S + 1 : ROW_S + 1 + C, :]
    north = halo_ref[ROW_N + 1 : ROW_N + 1 + C, :]

    def south_of(x, at):
        return jnp.where(first_row, pltpu.roll(south, -at % R, 1), pltpu.roll(x, 1, 1))

    def north_of(x, at):
        return jnp.where(last_row, pltpu.roll(north, (R - 1 - at) % R, 1), pltpu.roll(x, R - 1, 1))

    def shifted_south(edge, corner, at):
        spread = lax.broadcasted_iota(jnp.int32, edge.shape, 1)
        return jnp.where(spread == 0, pltpu.roll(corner, -at % R, 1), pltpu.roll(edge, 1, 1))

    def shifted_north(edge, corner, at):
        spread = lax.broadcasted_iota(jnp.int32, edge.shape, 1)
        return jnp.where(spread == R - 1, pltpu.roll(corner, (R - 1 - at) % R, 1),
                         pltpu.roll(edge, R - 1, 1))

    north_west, north_east = halo(ROW_N), halo(ROW_N + C + 1)
    south_east = halo(ROW_S + C + 1)
    b = b_ref[...].astype(jnp.float32)
    bw_edge, be_edge = halo(ROW_W + 97), halo(ROW_E + 96)
    b_w = west_of(b, bw_edge)
    b_e = east_of(b, be_edge)
    b_s = south_of(b, LANE_B + 1)
    b_n = north_of(b, LANE_B)
    b_nn = north_of(b_n, LANE_B + 1)
    b_nw = west_of(b_n, shifted_north(bw_edge, north_west, LANE_B))
    b_ne = east_of(b_n, shifted_north(be_edge, north_east, LANE_B))
    b_se = east_of(b_s, shifted_south(be_edge, south_east, LANE_B + 1))
    least = jnp.minimum
    d_u, d_v = least(b, b_e), least(b, b_n)
    d_vs = least(b, b_s)
    d_un, d_us = least(d_u, least(b_n, b_ne)), least(d_u, least(b_s, b_se))
    v_pairs = (least(d_v, least(b_e, b_ne)), least(d_v, least(b_w, b_nw)), least(d_v, b_nn),
               least(d_v, d_vs))

    base = (lax.axis_index("lat") * R + lane).astype(jnp.float32)
    cor_u = 2.0 * (base + 0.5) / rows_total - 1.0
    cor_v = 2.0 * (base + 1.0) / rows_total - 1.0

    zero = jnp.zeros((C, R), jnp.float32)
    sum_y = zero
    above = zero
    value = [zero] * 4
    outs = (t_out, s_out, u_out, v_out)

    for k in range(K):
        def keep(depth, x):
            return jnp.where(depth > k, x, 0.0)

        u = u_ref[k]
        v = v_ref[k]
        uw_edge = halo(ROW_W + 64 + k)
        vw_edge = halo(ROW_W + 80 + k)
        ve_edge = halo(ROW_E + 80 + k)
        u_s = south_of(u, LANE_U + k)
        u_n = north_of(u, LANE_U + k)
        v_w = west_of(v, vw_edge)
        v_e = east_of(v, ve_edge)
        v_s = south_of(v, LANE_V + k)
        v_n = north_of(v, LANE_V + k)

        fy = keep(d_v, v) * (1.0 / 12.0)
        fy_s = keep(d_vs, v_s) * (1.0 / 12.0)

        stars, norths, centres = [], [], []
        for part, ref, first in ((PART_T, t_ref, LANE_T), (PART_S, s_ref, LANE_S)):
            c = ref[k]
            at = first + 2 * k
            below = pltpu.roll(south, (R - 2 - at) % R, 1)
            c_s = pltpu.roll(jnp.where(last_row, below, c), 1, 1)
            c_ss = pltpu.roll(jnp.where(south_two, below, c), 2, 1)
            beyond = pltpu.roll(north, -at % R, 1)
            c_n = pltpu.roll(jnp.where(first_row, beyond, c), R - 1, 1)
            c_nn = pltpu.roll(jnp.where(north_two, beyond, c), R - 2, 1)
            advect = (
                fy_s * (7.0 * (c_s + c) - (c_ss + c_n)) - fy * (7.0 * (c + c_n) - (c_s + c_nn))
            )
            spread = keep(b_n, c_n - c) + keep(b_s, c_s - c)
            stars.append(c + keep(b, TIME_STEP * (part_ref[part, k] + (advect + TRACER_DIFF * spread))))
            centres.append(c)
            norths.append(c_n)

        def buoyancy(depth, pair):
            return keep(depth, THERMAL_EXPANSION * pair[0] - HALINE_CONTRACTION * pair[1])

        here = buoyancy(b, centres)
        step_y = buoyancy(b_n, norths) - here
        sum_y = sum_y + step_y

        pair_v = v + v_s
        edge_v = ve_edge + shifted_south(ve_edge, south_east, LANE_V + k)
        v_at_u = 0.25 * (pair_v + east_of(pair_v, edge_v))
        pair_u = u + u_n
        edge_u = uw_edge + shifted_north(uw_edge, north_west, LANE_U + k)
        u_at_v = 0.25 * (pair_u + west_of(pair_u, edge_u))
        u_visc = part_ref[PART_U, k] + (keep(d_un, u_n - u) + keep(d_us, u_s - u))
        v_visc = (keep(v_pairs[0], v_e - v) + keep(v_pairs[1], v_w - v)) + (
            keep(v_pairs[2], v_n - v) + keep(v_pairs[3], v_s - v))
        u_star = u + TIME_STEP * (
            cor_u * v_at_u - part_ref[PART_P, k] + MOMENTUM_VISC * u_visc)
        v_star = v + TIME_STEP * (
            -cor_v * u_at_v - (sum_y - 0.5 * step_y) + MOMENTUM_VISC * v_visc)
        if k == 0:
            u_star = u_star + TIME_STEP * WIND_GAIN * wind_ref[0]
            v_star = v_star + TIME_STEP * WIND_GAIN * wind_ref[1]
        coupling = zero if k == K - 1 else jnp.where(b > k + 1, TIME_STEP * mix_ref[k], 0.0)
        inv = part_ref[PART_INV, k]
        for index in range(2):
            value[index] = (stars[index] + above * value[index]) * inv
            outs[index][k] = value[index]
        above = coupling
        for index, depth, star in ((2, d_u, u_star), (3, d_v, v_star)):
            if k > 0:
                star = star + DRAG * value[index]
            if k < K - 1:
                star = star * jnp.where(depth > k + 1, INNER[k], LAST[k])
            else:
                star = star * LAST[k]
            value[index] = keep(depth, star)
            outs[index][k] = value[index]

    result = list(value)
    for k in range(K - 2, -1, -1):
        for index in range(4):
            if index < 2:
                result[index] = outs[index][k] - part_ref[PART_RATIO, k] * result[index]
            else:
                result[index] = outs[index][k] + (DRAG * INNER[k]) * result[index]
            outs[index][k] = result[index]


def shards(thermal_anomaly, saltiness_anomaly, zonal_current, meridional_current,
           bottom_ocean_layer, seam_axis_meridian, interface_diffusivity, atmospheric_forcing):
    n_lon = lax.axis_size("lon")
    n_lat = lax.axis_size("lat")
    n_y = 8 if n_lon >= 64 else n_lon // 2
    n_g = n_lon // n_y
    fields = (thermal_anomaly, saltiness_anomaly, zonal_current, meridional_current)
    vmem = pl.BlockSpec(memory_space=pltpu.VMEM)
    f32 = jnp.float32

    def exchange_body(*refs):
        exchange_kernel(n_lon, n_lat, n_y, *refs)

    def step_body(*refs):
        step_kernel(R * n_lat, *refs)

    halo, part = pl.pallas_call(
        exchange_body,
        name="exchange",
        out_shape=(jax.ShapeDtypeStruct((HALO_ROWS, R), f32),
                   jax.ShapeDtypeStruct((PARTS, K, C, R), f32)),
        in_specs=[pl.BlockSpec(memory_space=pltpu.HBM)] * 7,
        out_specs=(vmem, vmem),
        scratch_shapes=[
            pltpu.SMEM((1,), jnp.int32),
            *[pltpu.VMEM((K * C, R), f32) for _ in range(4)],
            pltpu.VMEM((C, R), jnp.int32),
            pltpu.VMEM((K - 1, C, R), f32),
            pltpu.VMEM((2, LON_ROWS, R), f32),
            pltpu.VMEM((2, LON_ROWS, R), f32),
            pltpu.VMEM((2, C, R), f32),
            pltpu.VMEM((6, C, R), f32),
            pltpu.VMEM((n_y * C, R), f32),
            pltpu.VMEM((n_g * 16, R), f32),
            pltpu.SemaphoreType.DMA((7,)),
            pltpu.SemaphoreType.DMA((2, 2)),
            pltpu.SemaphoreType.DMA((2, 6)),
            pltpu.SemaphoreType.DMA((2, n_y - 1)),
            pltpu.SemaphoreType.DMA((2, n_g - 1)),
        ],
        compiler_params=pltpu.CompilerParams(collective_id=0, has_side_effects=True,
                                             vmem_limit_bytes=4 << 20),
    )(seam_axis_meridian, *[
        pltpu.with_memory_space_constraint(operand, pltpu.HBM)
        for operand in (*[field.reshape(K * C, R) for field in fields], bottom_ocean_layer,
                        interface_diffusivity)
    ])
    return pl.pallas_call(
        step_body,
        name="step",
        out_shape=tuple(jax.ShapeDtypeStruct((K, C, R), f32) for _ in range(4)),
        in_specs=[vmem] * 9,
        out_specs=(vmem,) * 4,
        compiler_params=pltpu.CompilerParams(vmem_limit_bytes=4 << 20),
    )(*fields, bottom_ocean_layer, interface_diffusivity, atmospheric_forcing, halo,
      part)


def solution(mesh):
    grid = P(None, "lon", "lat")
    return jax.shard_map(
        shards,
        mesh=mesh,
        in_specs=(grid, grid, grid, grid, P("lon", "lat"), P(), grid, grid),
        out_specs=(grid,) * 4,
        check_vma=False,
    )
```

```python
import jax
import jax.numpy as jnp
from jax import lax
from jax.experimental import pallas as pl
from jax.experimental.pallas import tpu as pltpu
from jax.sharding import PartitionSpec as P

TIME_STEP = 0.2
TRACER_DIFF = 0.2
MOMENTUM_VISC = 0.2
THERMAL_EXPANSION = 0.5
HALINE_CONTRACTION = 0.4
WIND_GAIN = 2.0
VERTICAL_VISC = 1.0

K = 16
C = 8
R = 128

LANE_T, LANE_S, LANE_U, LANE_V, LANE_B = 0, 32, 64, 80, 96

LON_ROWS = 104
ROW_W, ROW_E = 0, LON_ROWS
ROW_S, ROW_N = 2 * LON_ROWS, 2 * LON_ROWS + 16
ROW_UN, ROW_VS = 2 * LON_ROWS + 32, 2 * LON_ROWS + 48
HALO_ROWS = 2 * LON_ROWS + 64


DRAG = TIME_STEP * VERTICAL_VISC
INNER, LAST = [], []
for _k in range(K):
    _above = DRAG * (1.0 - DRAG * INNER[-1]) if _k else 0.0
    INNER.append(1.0 / (1.0 + _above + DRAG))
    LAST.append(1.0 / (1.0 + _above))


def pack_rows(fields, depth, pair, single):
    lane = lax.broadcasted_iota(jnp.int32, (C, R), 1)
    half = lane // 2
    out = jnp.zeros((C, R), jnp.float32)
    for field, first in zip(fields[:2], (LANE_T, LANE_S)):
        for k in range(K):
            at = first + 2 * k
            moved = pltpu.roll(field[k * C : (k + 1) * C, :], (at - pair) % R, 1)
            out = jnp.where(half == at // 2, moved, out)
    for field, first in zip(fields[2:], (LANE_U, LANE_V)):
        for k in range(K):
            at = first + k
            moved = pltpu.roll(field[k * C : (k + 1) * C, :], (at - single) % R, 1)
            out = jnp.where(lane == at, moved, out)
    moved = pltpu.roll(depth, (LANE_B - pair) % R, 1)
    return jnp.where(half == LANE_B // 2, moved, out)


PART_T, PART_S, PART_P, PART_U, PART_INV, PART_RATIO = 0, 1, 2, 3, 4, 5
SHIFT_T, SHIFT_S, SHIFT_U, SHIFT_V, PARTS = 6, 10, 14, 16, 18


def east_west(t_ref, s_ref, u_ref, b, mix_ref, halo_ref, part_ref):
    sub = lax.broadcasted_iota(jnp.int32, (C, R), 0)
    first_col, last_col = sub == 0, sub == C - 1

    def halo(at):
        return jnp.broadcast_to(halo_ref[at : at + 1, :], (C, R))

    def west_of(x, edge):
        return jnp.where(first_col, edge, pltpu.roll(x, 1, 0))

    def east_of(x, edge):
        return jnp.where(last_col, edge, pltpu.roll(x, C - 1, 0))

    b_w = west_of(b, halo(ROW_W + 97))
    b_e = east_of(b, halo(ROW_E + 96))
    b_ee = east_of(b_e, halo(ROW_E + 97))
    d_u, d_uw = jnp.minimum(b, b_e), jnp.minimum(b, b_w)
    d_ue, d_uww = jnp.minimum(d_u, b_ee), jnp.minimum(d_uw, d_u)
    zero = jnp.zeros((C, R), jnp.float32)
    total, above, ratio = zero, zero, zero
    for k in range(K):
        def keep(depth, x):
            return jnp.where(depth > k, x, 0.0)

        def level(ref):
            return ref[k * C : (k + 1) * C, :]

        u = level(u_ref)
        u_w = west_of(u, halo(ROW_W + 64 + k))
        u_e = east_of(u, halo(ROW_E + 64 + k))
        fx = keep(d_u, u) * (1.0 / 12.0)
        fx_w = keep(d_uw, u_w) * (1.0 / 12.0)
        here, there = [], []
        for part, ref, block in ((PART_T, t_ref, 0), (PART_S, s_ref, 32)):
            c = level(ref)
            c_w = west_of(c, halo(ROW_W + block + 16 + k))
            c_ww = west_of(c_w, halo(ROW_W + block + k))
            c_e = east_of(c, halo(ROW_E + block + k))
            c_ee = east_of(c_e, halo(ROW_E + block + 16 + k))
            advect = (
                fx_w * (7.0 * (c_w + c) - (c_ww + c_e)) - fx * (7.0 * (c + c_e) - (c_w + c_ee))
            )
            part_ref[part, k] = advect + TRACER_DIFF * (keep(b_e, c_e - c) + keep(b_w, c_w - c))
            here.append(c)
            there.append(c_e)

        def buoyancy(depth, pair):
            return keep(depth, THERMAL_EXPANSION * pair[0] - HALINE_CONTRACTION * pair[1])

        change = buoyancy(b_e, there) - buoyancy(b, here)
        total = total + change
        part_ref[PART_P, k] = total - 0.5 * change
        part_ref[PART_U, k] = keep(d_ue, u_e - u) + keep(d_uww, u_w - u)
        coupling = zero if k == K - 1 else jnp.where(b > k + 1, TIME_STEP * mix_ref[k], 0.0)
        inv = 1.0 / (1.0 + coupling + above * (1.0 + ratio))
        above, ratio = coupling, -coupling * inv
        part_ref[PART_INV, k] = inv
        part_ref[PART_RATIO, k] = ratio


def exchange_kernel(n_lon, n_lat, n_y, q_any, t_any, s_any, u_any, v_any, b_any, mix_any,
                    out_ref, part_ref, q_ref, t_ref, s_ref, u_ref, v_ref, b_ref, mix_ref,
                    lon_out, lon_in, lat_out, lat_in, tiles, windows,
                    load_sems, lon_sems, lat_sems, low_sems, high_sems):
    n_g = n_lon // n_y
    lon = lax.axis_index("lon")
    lat = lax.axis_index("lat")
    group = lon // n_y
    low = lon % n_y
    east = (lon + 1) % n_lon
    west = (lon + n_lon - 1) % n_lon
    is_top = lat == n_lat - 1
    has_north = lat < n_lat - 1
    has_south = lat > 0
    sides = (west, lon, east)

    def device(lon_at, lat_at):
        return {"lon": lon_at, "lat": lat_at}

    barrier = pltpu.get_barrier_semaphore()

    def greet(lon_at, lat_at):
        pl.semaphore_signal(barrier, inc=1, device_id=device(lon_at, lat_at),
                            device_id_type=pl.DeviceIdType.MESH)

    low_peers = [group * n_y + (low + d) % n_y for d in range(1, n_y)]
    high_peers = [((group + d) % n_g) * n_y + low for d in range(1, n_g)]

    @pl.when(is_top)
    def _():
        for peer in low_peers + high_peers:
            greet(peer, lat)

    loads = [
        pltpu.make_async_copy(source, target, load_sems.at[at])
        for at, (source, target) in enumerate(
            zip((q_any, t_any, s_any, u_any, v_any, b_any),
                (q_ref, t_ref, s_ref, u_ref, v_ref, b_ref)))
    ]
    for load in loads:
        load.start()
    mix_load = pltpu.make_async_copy(mix_any, mix_ref, load_sems.at[6])
    mix_load.start()

    greet(west, lat)
    greet(east, lat)

    @pl.when(has_north)
    def _():
        for side in sides:
            greet(side, lat + 1)

    @pl.when(has_south)
    def _():
        for side in sides:
            greet(side, lat - 1)

    for load in loads:
        load.wait()
    fields = (t_ref, s_ref, u_ref, v_ref)
    depth = b_ref[...].astype(jnp.float32)

    def column(ref, at):
        return ref[pl.ds(at, K, stride=C), :]

    def pack_columns():
        for slot, cols in ((0, (C - 2, C - 1)), (1, (0, 1))):
            near = cols[1] if slot == 0 else cols[0]
            lon_out[slot, 0:16, :] = column(t_ref, cols[0])
            lon_out[slot, 16:32, :] = column(t_ref, cols[1])
            lon_out[slot, 32:48, :] = column(s_ref, cols[0])
            lon_out[slot, 48:64, :] = column(s_ref, cols[1])
            lon_out[slot, 64:80, :] = column(u_ref, near)
            lon_out[slot, 80:96, :] = column(v_ref, near)
            rolled = depth if slot == 1 else pltpu.roll(depth, 2, 0)
            lon_out[slot, 96:104, :] = rolled

    def pack_south():
        lat_out[1] = pack_rows(fields, depth, 0, 0)

    upper = pack_rows(fields, depth, R - 2, R - 1)
    lat_out[0] = upper
    q = q_ref[0]

    @pl.when(is_top)
    def _():
        lower = pack_rows(fields, depth, R - 3, R - 2)
        chosen = jnp.where((q & 1) == 1, upper, lower)
        lane = lax.broadcasted_iota(jnp.int32, (C, R), 1)
        swapped = jnp.where(lane % 2 == 0, pltpu.roll(chosen, R - 1, 1), pltpu.roll(chosen, 1, 1))
        currents = jnp.logical_and(lane >= LANE_U, lane < LANE_B)
        tiles[pl.ds(pl.multiple_of(low * C, C), C), :] = jnp.where(currents, -chosen, swapped)

    @pl.when(jnp.logical_not(is_top))
    def _():
        pack_south()
        pack_columns()

    lat_greets = jnp.where(has_north, 3, 0) + jnp.where(has_south, 3, 0)
    top_greets = jnp.where(is_top, n_y - 1 + n_g - 1, 0)
    pl.semaphore_wait(barrier, 2 + lat_greets + top_greets)

    def low_copy(d):
        mine = tiles.at[pl.ds(pl.multiple_of(low * C, C), C), :]
        return pltpu.make_async_remote_copy(
            src_ref=mine, dst_ref=mine, send_sem=low_sems.at[0, d - 1],
            recv_sem=low_sems.at[1, d - 1], device_id=device(low_peers[d - 1], lat),
            device_id_type=pl.DeviceIdType.MESH)

    def high_copy(d):
        mine = windows.at[pl.ds(pl.multiple_of(group * 16, 16), 16), :]
        return pltpu.make_async_remote_copy(
            src_ref=mine, dst_ref=mine, send_sem=high_sems.at[0, d - 1],
            recv_sem=high_sems.at[1, d - 1], device_id=device(high_peers[d - 1], lat),
            device_id_type=pl.DeviceIdType.MESH)

    @pl.when(is_top)
    def _():
        for d in range(1, n_y):
            low_copy(d).start()
        pack_south()

    def lon_copy(slot):
        return pltpu.make_async_remote_copy(
            src_ref=lon_out.at[slot], dst_ref=lon_in.at[slot], send_sem=lon_sems.at[0, slot],
            recv_sem=lon_sems.at[1, slot], device_id=device((east, west)[slot], lat),
            device_id_type=pl.DeviceIdType.MESH)

    def lat_copy(direction, side):
        slot = 3 * direction + 2 - side
        return pltpu.make_async_remote_copy(
            src_ref=lat_out.at[direction], dst_ref=lat_in.at[slot],
            send_sem=lat_sems.at[0, slot], recv_sem=lat_sems.at[1, slot],
            device_id=device(sides[side], lat + 1 if direction == 0 else lat - 1),
            device_id_type=pl.DeviceIdType.MESH)

    @pl.when(has_north)
    def _():
        for side in range(3):
            lat_copy(0, side).start()

    @pl.when(has_south)
    def _():
        for side in range(3):
            lat_copy(1, side).start()

    @pl.when(jnp.logical_not(is_top))
    def _():
        for slot in range(2):
            lon_copy(slot).start()

    @pl.when(is_top)
    def _():
        pack_columns()

    for k in range(K):
        for ref, first, shifts in ((t_ref, SHIFT_T, (1, 2, -1, -2)), (s_ref, SHIFT_S, (1, 2, -1, -2)),
                                   (u_ref, SHIFT_U, (1, -1)), (v_ref, SHIFT_V, (1, -1))):
            for at, shift in enumerate(shifts):
                part_ref[first + at, k] = pltpu.roll(ref[k * C : (k + 1) * C, :], shift % R, 1)

    row = lax.broadcasted_iota(jnp.int32, (16, R), 0)

    def assemble(get):
        out = jnp.zeros((16, R), jnp.float32)
        for index in range(C + 2):
            out = jnp.where(row == index, get(index), out)
        return out

    @pl.when(is_top)
    def _():
        for d in range(1, n_y):
            low_copy(d).wait_recv()
        span = n_y * C

        def near(index):
            at = (q - C * low - (index - 1) + 4 * n_lon * C) & (span - 1)
            return tiles[pl.ds(at, 1), :]

        windows[pl.ds(pl.multiple_of(group * 16, 16), 16), :] = assemble(near)
        for d in range(1, n_g):
            high_copy(d).start()
        for slot in range(2):
            lon_copy(slot).start()

    for slot in range(2):
        lon_copy(slot).wait_recv()
    out_ref[ROW_W : ROW_W + LON_ROWS, :] = lon_in[0]
    out_ref[ROW_E : ROW_E + LON_ROWS, :] = lon_in[1]
    out_ref[ROW_UN : ROW_UN + 16, :] = pltpu.roll(lon_in[0, 64:80, :], R - 1, 1)
    out_ref[ROW_VS : ROW_VS + 16, :] = pltpu.roll(lon_in[1, 80:96, :], 1, 1)
    mix_load.wait()
    east_west(t_ref, s_ref, u_ref, depth, mix_ref, out_ref, part_ref)

    def side_rows(first):
        def get(index):
            if index == 0:
                return lat_in[first, C - 1 : C, :]
            if index == C + 1:
                return lat_in[first + 2, 0:1, :]
            return lat_in[first + 1, index - 1 : index, :]

        return assemble(get)

    @pl.when(has_south)
    def _():
        for side in range(3):
            lat_copy(0, 2 - side).wait_recv()
        out_ref[ROW_S : ROW_S + 16, :] = side_rows(0)

    @pl.when(jnp.logical_not(has_south))
    def _():
        out_ref[ROW_S : ROW_S + 16, :] = jnp.zeros((16, R), jnp.float32)

    @pl.when(has_north)
    def _():
        for side in range(3):
            lat_copy(1, 2 - side).wait_recv()
        out_ref[ROW_N : ROW_N + 16, :] = side_rows(3)

    @pl.when(is_top)
    def _():
        for d in range(1, n_g):
            high_copy(d).wait_recv()
        span = n_y * C

        def far(index):
            at = (q - C * lon - (index - 1) + 4 * n_lon * C) & (n_lon * C - 1)
            return windows[pl.ds(lax.shift_right_logical(at, span.bit_length() - 1) * 16 + index, 1), :]

        out_ref[ROW_N : ROW_N + 16, :] = assemble(far)
        for d in range(1, n_y):
            low_copy(d).wait_send()
        for d in range(1, n_g):
            high_copy(d).wait_send()

    for slot in range(2):
        lon_copy(slot).wait_send()

    @pl.when(has_north)
    def _():
        for side in range(3):
            lat_copy(0, side).wait_send()

    @pl.when(has_south)
    def _():
        for side in range(3):
            lat_copy(1, side).wait_send()


def step_kernel(rows_total, t_ref, s_ref, u_ref, v_ref, b_ref, mix_ref, wind_ref, halo_ref, part_ref,
                t_out, s_out, u_out, v_out):
    sub = lax.broadcasted_iota(jnp.int32, (C, R), 0)
    lane = lax.broadcasted_iota(jnp.int32, (C, R), 1)
    first_col, last_col = sub == 0, sub == C - 1
    first_row, last_row = lane == 0, lane == R - 1
    south_two, north_two = lane >= R - 2, lane < 2

    def halo(at):
        return jnp.broadcast_to(halo_ref[at : at + 1, :], (C, R))

    def west_of(x, edge):
        return jnp.where(first_col, edge, pltpu.roll(x, 1, 0))

    def east_of(x, edge):
        return jnp.where(last_col, edge, pltpu.roll(x, C - 1, 0))

    south = halo_ref[ROW_S + 1 : ROW_S + 1 + C, :]
    north = halo_ref[ROW_N + 1 : ROW_N + 1 + C, :]

    def south_edge(shifted, at):
        return jnp.where(first_row, pltpu.roll(south, -at % R, 1), shifted)

    def north_edge(shifted, at):
        return jnp.where(last_row, pltpu.roll(north, (R - 1 - at) % R, 1), shifted)

    def south_of(x, at):
        return jnp.where(first_row, pltpu.roll(south, -at % R, 1), pltpu.roll(x, 1, 1))

    def north_of(x, at):
        return jnp.where(last_row, pltpu.roll(north, (R - 1 - at) % R, 1), pltpu.roll(x, R - 1, 1))

    def shifted_south(edge, corner, at):
        spread = lax.broadcasted_iota(jnp.int32, edge.shape, 1)
        return jnp.where(spread == 0, pltpu.roll(corner, -at % R, 1), pltpu.roll(edge, 1, 1))

    def shifted_north(edge, corner, at):
        spread = lax.broadcasted_iota(jnp.int32, edge.shape, 1)
        return jnp.where(spread == R - 1, pltpu.roll(corner, (R - 1 - at) % R, 1),
                         pltpu.roll(edge, R - 1, 1))

    north_west, north_east = halo(ROW_N), halo(ROW_N + C + 1)
    south_east = halo(ROW_S + C + 1)
    b = b_ref[...].astype(jnp.float32)
    bw_edge, be_edge = halo(ROW_W + 97), halo(ROW_E + 96)
    b_w = west_of(b, bw_edge)
    b_e = east_of(b, be_edge)
    b_s = south_of(b, LANE_B + 1)
    b_n = north_of(b, LANE_B)
    b_nn = north_of(b_n, LANE_B + 1)
    b_nw = west_of(b_n, shifted_north(bw_edge, north_west, LANE_B))
    b_ne = east_of(b_n, shifted_north(be_edge, north_east, LANE_B))
    b_se = east_of(b_s, shifted_south(be_edge, south_east, LANE_B + 1))
    least = jnp.minimum
    d_u, d_v = least(b, b_e), least(b, b_n)
    d_vs = least(b, b_s)
    d_un, d_us = least(d_u, least(b_n, b_ne)), least(d_u, least(b_s, b_se))
    v_pairs = (least(d_v, least(b_e, b_ne)), least(d_v, least(b_w, b_nw)), least(d_v, b_nn),
               least(d_v, d_vs))

    base = (lax.axis_index("lat") * R + lane).astype(jnp.float32)
    cor_u = 2.0 * (base + 0.5) / rows_total - 1.0
    cor_v = 2.0 * (base + 1.0) / rows_total - 1.0

    zero = jnp.zeros((C, R), jnp.float32)
    sum_y = zero
    above = zero
    value = [zero] * 4
    outs = (t_out, s_out, u_out, v_out)

    for k in range(K):
        def keep(depth, x):
            return jnp.where(depth > k, x, 0.0)

        u = u_ref[k]
        v = v_ref[k]
        uw_edge = halo(ROW_W + 64 + k)
        vw_edge = halo(ROW_W + 80 + k)
        ve_edge = halo(ROW_E + 80 + k)
        u_s = south_edge(part_ref[SHIFT_U, k], LANE_U + k)
        u_n = north_edge(part_ref[SHIFT_U + 1, k], LANE_U + k)
        v_w = west_of(v, vw_edge)
        v_e = east_of(v, ve_edge)
        v_s = south_edge(part_ref[SHIFT_V, k], LANE_V + k)
        v_n = north_edge(part_ref[SHIFT_V + 1, k], LANE_V + k)

        fy = keep(d_v, v) * (1.0 / 12.0)
        fy_s = keep(d_vs, v_s) * (1.0 / 12.0)

        stars, norths, centres = [], [], []
        for part, shift, ref, first in ((PART_T, SHIFT_T, t_ref, LANE_T),
                                        (PART_S, SHIFT_S, s_ref, LANE_S)):
            c = ref[k]
            at = first + 2 * k
            c_s = south_edge(part_ref[shift, k], at + 1)
            c_ss = jnp.where(north_two, pltpu.roll(south, -at % R, 1), part_ref[shift + 1, k])
            c_n = north_edge(part_ref[shift + 2, k], at)
            c_nn = jnp.where(south_two, pltpu.roll(north, (R - 2 - at) % R, 1),
                             part_ref[shift + 3, k])
            advect = (
                fy_s * (7.0 * (c_s + c) - (c_ss + c_n)) - fy * (7.0 * (c + c_n) - (c_s + c_nn))
            )
            spread = keep(b_n, c_n - c) + keep(b_s, c_s - c)
            stars.append(c + keep(b, TIME_STEP * (part_ref[part, k] + (advect + TRACER_DIFF * spread))))
            centres.append(c)
            norths.append(c_n)

        def buoyancy(depth, pair):
            return keep(depth, THERMAL_EXPANSION * pair[0] - HALINE_CONTRACTION * pair[1])

        here = buoyancy(b, centres)
        step_y = buoyancy(b_n, norths) - here
        sum_y = sum_y + step_y

        pair_v = v + v_s
        edge_v = ve_edge + jnp.where(
            first_row, pltpu.roll(south_east, -(LANE_V + k) % R, 1), halo(ROW_VS + k))
        v_at_u = 0.25 * (pair_v + east_of(pair_v, edge_v))
        pair_u = u + u_n
        edge_u = uw_edge + jnp.where(
            last_row, pltpu.roll(north_west, (R - 1 - LANE_U - k) % R, 1), halo(ROW_UN + k))
        u_at_v = 0.25 * (pair_u + west_of(pair_u, edge_u))
        u_visc = part_ref[PART_U, k] + (keep(d_un, u_n - u) + keep(d_us, u_s - u))
        v_visc = (keep(v_pairs[0], v_e - v) + keep(v_pairs[1], v_w - v)) + (
            keep(v_pairs[2], v_n - v) + keep(v_pairs[3], v_s - v))
        u_star = u + TIME_STEP * (
            cor_u * v_at_u - part_ref[PART_P, k] + MOMENTUM_VISC * u_visc)
        v_star = v + TIME_STEP * (
            -cor_v * u_at_v - (sum_y - 0.5 * step_y) + MOMENTUM_VISC * v_visc)
        if k == 0:
            u_star = u_star + TIME_STEP * WIND_GAIN * wind_ref[0]
            v_star = v_star + TIME_STEP * WIND_GAIN * wind_ref[1]
        coupling = zero if k == K - 1 else jnp.where(b > k + 1, TIME_STEP * mix_ref[k], 0.0)
        inv = part_ref[PART_INV, k]
        for index in range(2):
            value[index] = (stars[index] + above * value[index]) * inv
            outs[index][k] = value[index]
        above = coupling
        for index, depth, star in ((2, d_u, u_star), (3, d_v, v_star)):
            if k > 0:
                star = star + DRAG * value[index]
            if k < K - 1:
                star = star * jnp.where(depth > k + 1, INNER[k], LAST[k])
            else:
                star = star * LAST[k]
            value[index] = keep(depth, star)
            outs[index][k] = value[index]

    result = list(value)
    for k in range(K - 2, -1, -1):
        for index in range(4):
            if index < 2:
                result[index] = outs[index][k] - part_ref[PART_RATIO, k] * result[index]
            else:
                result[index] = outs[index][k] + (DRAG * INNER[k]) * result[index]
            outs[index][k] = result[index]


def shards(thermal_anomaly, saltiness_anomaly, zonal_current, meridional_current,
           bottom_ocean_layer, seam_axis_meridian, interface_diffusivity, atmospheric_forcing):
    n_lon = lax.axis_size("lon")
    n_lat = lax.axis_size("lat")
    n_y = 8 if n_lon >= 64 else n_lon // 2
    n_g = n_lon // n_y
    fields = (thermal_anomaly, saltiness_anomaly, zonal_current, meridional_current)
    vmem = pl.BlockSpec(memory_space=pltpu.VMEM)
    f32 = jnp.float32

    def exchange_body(*refs):
        exchange_kernel(n_lon, n_lat, n_y, *refs)

    def step_body(*refs):
        step_kernel(R * n_lat, *refs)

    halo, part = pl.pallas_call(
        exchange_body,
        name="exchange",
        out_shape=(jax.ShapeDtypeStruct((HALO_ROWS, R), f32),
                   jax.ShapeDtypeStruct((PARTS, K, C, R), f32)),
        in_specs=[pl.BlockSpec(memory_space=pltpu.HBM)] * 7,
        out_specs=(vmem, vmem),
        scratch_shapes=[
            pltpu.SMEM((1,), jnp.int32),
            *[pltpu.VMEM((K * C, R), f32) for _ in range(4)],
            pltpu.VMEM((C, R), jnp.int32),
            pltpu.VMEM((K - 1, C, R), f32),
            pltpu.VMEM((2, LON_ROWS, R), f32),
            pltpu.VMEM((2, LON_ROWS, R), f32),
            pltpu.VMEM((2, C, R), f32),
            pltpu.VMEM((6, C, R), f32),
            pltpu.VMEM((n_y * C, R), f32),
            pltpu.VMEM((n_g * 16, R), f32),
            pltpu.SemaphoreType.DMA((7,)),
            pltpu.SemaphoreType.DMA((2, 2)),
            pltpu.SemaphoreType.DMA((2, 6)),
            pltpu.SemaphoreType.DMA((2, n_y - 1)),
            pltpu.SemaphoreType.DMA((2, n_g - 1)),
        ],
        compiler_params=pltpu.CompilerParams(collective_id=0, has_side_effects=True,
                                             vmem_limit_bytes=4 << 20),
    )(seam_axis_meridian, *[
        pltpu.with_memory_space_constraint(operand, pltpu.HBM)
        for operand in (*[field.reshape(K * C, R) for field in fields], bottom_ocean_layer,
                        interface_diffusivity)
    ])
    return pl.pallas_call(
        step_body,
        name="step",
        out_shape=tuple(jax.ShapeDtypeStruct((K, C, R), f32) for _ in range(4)),
        in_specs=[vmem] * 9,
        out_specs=(vmem,) * 4,
        compiler_params=pltpu.CompilerParams(vmem_limit_bytes=4 << 20),
    )(*fields, bottom_ocean_layer, interface_diffusivity, atmospheric_forcing, halo,
      part)


def solution(mesh):
    grid = P(None, "lon", "lat")
    return jax.shard_map(
        shards,
        mesh=mesh,
        in_specs=(grid, grid, grid, grid, P("lon", "lat"), P(), grid, grid),
        out_specs=(grid,) * 4,
        check_vma=False,
    )
```

```python
import jax
import jax.numpy as jnp
from jax import lax
from jax.experimental import pallas as pl
from jax.experimental.pallas import tpu as pltpu
from jax.sharding import PartitionSpec as P

TIME_STEP = 0.2
TRACER_DIFF = 0.2
MOMENTUM_VISC = 0.2
THERMAL_EXPANSION = 0.5
HALINE_CONTRACTION = 0.4
WIND_GAIN = 2.0
VERTICAL_VISC = 1.0

K = 16
C = 8
R = 128

LANE_T, LANE_S, LANE_U, LANE_V, LANE_B = 0, 32, 64, 80, 96

LON_ROWS = 104
ROW_W, ROW_E = 0, LON_ROWS
ROW_S, ROW_N = 2 * LON_ROWS, 2 * LON_ROWS + 16
ROW_UN, ROW_VS = 2 * LON_ROWS + 32, 2 * LON_ROWS + 48
HALO_ROWS = 2 * LON_ROWS + 64


DRAG = TIME_STEP * VERTICAL_VISC
INNER, LAST = [], []
for _k in range(K):
    _above = DRAG * (1.0 - DRAG * INNER[-1]) if _k else 0.0
    INNER.append(1.0 / (1.0 + _above + DRAG))
    LAST.append(1.0 / (1.0 + _above))


def pack_rows(fields, depth, pair, single):
    lane = lax.broadcasted_iota(jnp.int32, (C, R), 1)
    half = lane // 2
    out = jnp.zeros((C, R), jnp.float32)
    for field, first in zip(fields[:2], (LANE_T, LANE_S)):
        for k in range(K):
            at = first + 2 * k
            moved = pltpu.roll(field[k * C : (k + 1) * C, :], (at - pair) % R, 1)
            out = jnp.where(half == at // 2, moved, out)
    for field, first in zip(fields[2:], (LANE_U, LANE_V)):
        for k in range(K):
            at = first + k
            moved = pltpu.roll(field[k * C : (k + 1) * C, :], (at - single) % R, 1)
            out = jnp.where(lane == at, moved, out)
    moved = pltpu.roll(depth, (LANE_B - pair) % R, 1)
    return jnp.where(half == LANE_B // 2, moved, out)


PART_T, PART_S, PART_P, PART_U, PART_INV, PART_RATIO = 0, 1, 2, 3, 4, 5
SHIFT_T, SHIFT_S, SHIFT_U, SHIFT_V, PARTS = 6, 10, 14, 16, 18


def east_west(t_ref, s_ref, u_ref, b, mix_ref, halo_ref, part_ref):
    sub = lax.broadcasted_iota(jnp.int32, (C, R), 0)
    first_col, last_col = sub == 0, sub == C - 1

    def halo(at):
        return jnp.broadcast_to(halo_ref[at : at + 1, :], (C, R))

    def west_of(x, edge):
        return jnp.where(first_col, edge, pltpu.roll(x, 1, 0))

    def east_of(x, edge):
        return jnp.where(last_col, edge, pltpu.roll(x, C - 1, 0))

    b_w = west_of(b, halo(ROW_W + 97))
    b_e = east_of(b, halo(ROW_E + 96))
    b_ee = east_of(b_e, halo(ROW_E + 97))
    d_u, d_uw = jnp.minimum(b, b_e), jnp.minimum(b, b_w)
    d_ue, d_uww = jnp.minimum(d_u, b_ee), jnp.minimum(d_uw, d_u)
    zero = jnp.zeros((C, R), jnp.float32)
    total, above, ratio = zero, zero, zero
    for k in range(K):
        def keep(depth, x):
            return jnp.where(depth > k, x, 0.0)

        def level(ref):
            return ref[k * C : (k + 1) * C, :]

        u = level(u_ref)
        u_w = west_of(u, halo(ROW_W + 64 + k))
        u_e = east_of(u, halo(ROW_E + 64 + k))
        fx = keep(d_u, u) * (1.0 / 12.0)
        fx_w = keep(d_uw, u_w) * (1.0 / 12.0)
        here, there = [], []
        for part, ref, block in ((PART_T, t_ref, 0), (PART_S, s_ref, 32)):
            c = level(ref)
            c_w = west_of(c, halo(ROW_W + block + 16 + k))
            c_ww = west_of(c_w, halo(ROW_W + block + k))
            c_e = east_of(c, halo(ROW_E + block + k))
            c_ee = east_of(c_e, halo(ROW_E + block + 16 + k))
            advect = (
                fx_w * (7.0 * (c_w + c) - (c_ww + c_e)) - fx * (7.0 * (c + c_e) - (c_w + c_ee))
            )
            part_ref[part, k] = advect + TRACER_DIFF * (keep(b_e, c_e - c) + keep(b_w, c_w - c))
            here.append(c)
            there.append(c_e)

        def buoyancy(depth, pair):
            return keep(depth, THERMAL_EXPANSION * pair[0] - HALINE_CONTRACTION * pair[1])

        change = buoyancy(b_e, there) - buoyancy(b, here)
        total = total + change
        part_ref[PART_P, k] = total - 0.5 * change
        part_ref[PART_U, k] = keep(d_ue, u_e - u) + keep(d_uww, u_w - u)
        coupling = zero if k == K - 1 else jnp.where(b > k + 1, TIME_STEP * mix_ref[k], 0.0)
        inv = 1.0 / (1.0 + coupling + above * (1.0 + ratio))
        above, ratio = coupling, -coupling * inv
        part_ref[PART_INV, k] = inv
        part_ref[PART_RATIO, k] = ratio


def exchange_kernel(n_lon, n_lat, n_y, q_any, t_any, s_any, u_any, v_any, b_any, mix_any,
                    out_ref, part_ref, q_ref, t_ref, s_ref, u_ref, v_ref, b_ref, mix_ref,
                    lon_out, lon_in, lat_out, lat_in, tiles, windows,
                    load_sems, lon_sems, lat_sems, low_sems, high_sems):
    n_g = n_lon // n_y
    lon = lax.axis_index("lon")
    lat = lax.axis_index("lat")
    group = lon // n_y
    low = lon % n_y
    east = (lon + 1) % n_lon
    west = (lon + n_lon - 1) % n_lon
    is_top = lat == n_lat - 1
    has_north = lat < n_lat - 1
    has_south = lat > 0
    sides = (west, lon, east)

    def device(lon_at, lat_at):
        return {"lon": lon_at, "lat": lat_at}

    barrier = pltpu.get_barrier_semaphore()

    def greet(lon_at, lat_at):
        pl.semaphore_signal(barrier, inc=1, device_id=device(lon_at, lat_at),
                            device_id_type=pl.DeviceIdType.MESH)

    low_peers = [group * n_y + (low + d) % n_y for d in range(1, n_y)]
    high_peers = [((group + d) % n_g) * n_y + low for d in range(1, n_g)]

    @pl.when(is_top)
    def _():
        for peer in low_peers + high_peers:
            greet(peer, lat)

    loads = [
        pltpu.make_async_copy(source, target, load_sems.at[at])
        for at, (source, target) in enumerate(
            zip((q_any, t_any, s_any, u_any, v_any, b_any),
                (q_ref, t_ref, s_ref, u_ref, v_ref, b_ref)))
    ]
    for load in loads:
        load.start()
    mix_load = pltpu.make_async_copy(mix_any, mix_ref, load_sems.at[6])
    mix_load.start()

    greet(west, lat)
    greet(east, lat)

    @pl.when(has_north)
    def _():
        for side in sides:
            greet(side, lat + 1)

    @pl.when(has_south)
    def _():
        for side in sides:
            greet(side, lat - 1)

    for load in loads:
        load.wait()
    fields = (t_ref, s_ref, u_ref, v_ref)
    depth = b_ref[...].astype(jnp.float32)

    def column(ref, at):
        return ref[pl.ds(at, K, stride=C), :]

    def pack_columns():
        for slot, cols in ((0, (C - 2, C - 1)), (1, (0, 1))):
            near = cols[1] if slot == 0 else cols[0]
            lon_out[slot, 0:16, :] = column(t_ref, cols[0])
            lon_out[slot, 16:32, :] = column(t_ref, cols[1])
            lon_out[slot, 32:48, :] = column(s_ref, cols[0])
            lon_out[slot, 48:64, :] = column(s_ref, cols[1])
            lon_out[slot, 64:80, :] = column(u_ref, near)
            lon_out[slot, 80:96, :] = column(v_ref, near)
            rolled = depth if slot == 1 else pltpu.roll(depth, 2, 0)
            lon_out[slot, 96:104, :] = rolled

    def pack_south():
        lat_out[1] = pack_rows(fields, depth, 0, 0)

    upper = pack_rows(fields, depth, R - 2, R - 1)
    lat_out[0] = upper
    q = q_ref[0]

    @pl.when(is_top)
    def _():
        lower = pack_rows(fields, depth, R - 3, R - 2)
        chosen = jnp.where((q & 1) == 1, upper, lower)
        lane = lax.broadcasted_iota(jnp.int32, (C, R), 1)
        swapped = jnp.where(lane % 2 == 0, pltpu.roll(chosen, R - 1, 1), pltpu.roll(chosen, 1, 1))
        currents = jnp.logical_and(lane >= LANE_U, lane < LANE_B)
        tiles[pl.ds(pl.multiple_of(low * C, C), C), :] = jnp.where(currents, -chosen, swapped)

    @pl.when(jnp.logical_not(is_top))
    def _():
        pack_south()
        pack_columns()

    lat_greets = jnp.where(has_north, 3, 0) + jnp.where(has_south, 3, 0)
    top_greets = jnp.where(is_top, n_y - 1 + n_g - 1, 0)
    pl.semaphore_wait(barrier, 2 + lat_greets + top_greets)

    def low_copy(d):
        mine = tiles.at[pl.ds(pl.multiple_of(low * C, C), C), :]
        return pltpu.make_async_remote_copy(
            src_ref=mine, dst_ref=mine, send_sem=low_sems.at[0, d - 1],
            recv_sem=low_sems.at[1, d - 1], device_id=device(low_peers[d - 1], lat),
            device_id_type=pl.DeviceIdType.MESH)

    def high_copy(d):
        mine = windows.at[pl.ds(pl.multiple_of(group * 16, 16), 16), :]
        return pltpu.make_async_remote_copy(
            src_ref=mine, dst_ref=mine, send_sem=high_sems.at[0, d - 1],
            recv_sem=high_sems.at[1, d - 1], device_id=device(high_peers[d - 1], lat),
            device_id_type=pl.DeviceIdType.MESH)

    @pl.when(is_top)
    def _():
        for d in range(1, n_y):
            low_copy(d).start()
        pack_south()

    def lon_copy(slot):
        return pltpu.make_async_remote_copy(
            src_ref=lon_out.at[slot], dst_ref=lon_in.at[slot], send_sem=lon_sems.at[0, slot],
            recv_sem=lon_sems.at[1, slot], device_id=device((east, west)[slot], lat),
            device_id_type=pl.DeviceIdType.MESH)

    def lat_copy(direction, side):
        slot = 3 * direction + 2 - side
        return pltpu.make_async_remote_copy(
            src_ref=lat_out.at[direction], dst_ref=lat_in.at[slot],
            send_sem=lat_sems.at[0, slot], recv_sem=lat_sems.at[1, slot],
            device_id=device(sides[side], lat + 1 if direction == 0 else lat - 1),
            device_id_type=pl.DeviceIdType.MESH)

    @pl.when(has_north)
    def _():
        for side in range(3):
            lat_copy(0, side).start()

    @pl.when(has_south)
    def _():
        for side in range(3):
            lat_copy(1, side).start()

    @pl.when(jnp.logical_not(is_top))
    def _():
        for slot in range(2):
            lon_copy(slot).start()

    @pl.when(is_top)
    def _():
        pack_columns()

    for k in range(K):
        for ref, first, shifts in ((t_ref, SHIFT_T, (1, 2, -1, -2)), (s_ref, SHIFT_S, (1, 2, -1, -2)),
                                   (u_ref, SHIFT_U, (1, -1)), (v_ref, SHIFT_V, (1, -1))):
            for at, shift in enumerate(shifts):
                part_ref[first + at, k] = pltpu.roll(ref[k * C : (k + 1) * C, :], shift % R, 1)

    row = lax.broadcasted_iota(jnp.int32, (16, R), 0)

    def assemble(get):
        out = jnp.zeros((16, R), jnp.float32)
        for index in range(C + 2):
            out = jnp.where(row == index, get(index), out)
        return out

    @pl.when(is_top)
    def _():
        for d in range(1, n_y):
            low_copy(d).wait_recv()
        span = n_y * C

        def near(index):
            at = (q - C * low - (index - 1) + 4 * n_lon * C) & (span - 1)
            return tiles[pl.ds(at, 1), :]

        windows[pl.ds(pl.multiple_of(group * 16, 16), 16), :] = assemble(near)
        for d in range(1, n_g):
            high_copy(d).start()
        for slot in range(2):
            lon_copy(slot).start()

    for slot in range(2):
        lon_copy(slot).wait_recv()
    out_ref[ROW_W : ROW_W + LON_ROWS, :] = lon_in[0]
    out_ref[ROW_E : ROW_E + LON_ROWS, :] = lon_in[1]
    out_ref[ROW_UN : ROW_UN + 16, :] = pltpu.roll(lon_in[0, 64:80, :], R - 1, 1)
    out_ref[ROW_VS : ROW_VS + 16, :] = pltpu.roll(lon_in[1, 80:96, :], 1, 1)
    mix_load.wait()
    east_west(t_ref, s_ref, u_ref, depth, mix_ref, out_ref, part_ref)

    def side_rows(first):
        def get(index):
            if index == 0:
                return lat_in[first, C - 1 : C, :]
            if index == C + 1:
                return lat_in[first + 2, 0:1, :]
            return lat_in[first + 1, index - 1 : index, :]

        return assemble(get)

    @pl.when(has_south)
    def _():
        for side in range(3):
            lat_copy(0, 2 - side).wait_recv()
        out_ref[ROW_S : ROW_S + 16, :] = side_rows(0)

    @pl.when(jnp.logical_not(has_south))
    def _():
        out_ref[ROW_S : ROW_S + 16, :] = jnp.zeros((16, R), jnp.float32)

    @pl.when(has_north)
    def _():
        for side in range(3):
            lat_copy(1, 2 - side).wait_recv()
        out_ref[ROW_N : ROW_N + 16, :] = side_rows(3)

    @pl.when(is_top)
    def _():
        for d in range(1, n_g):
            high_copy(d).wait_recv()
        span = n_y * C

        def far(index):
            at = (q - C * lon - (index - 1) + 4 * n_lon * C) & (n_lon * C - 1)
            return windows[pl.ds(lax.shift_right_logical(at, span.bit_length() - 1) * 16 + index, 1), :]

        out_ref[ROW_N : ROW_N + 16, :] = assemble(far)
        for d in range(1, n_y):
            low_copy(d).wait_send()
        for d in range(1, n_g):
            high_copy(d).wait_send()

    for slot in range(2):
        lon_copy(slot).wait_send()

    @pl.when(has_north)
    def _():
        for side in range(3):
            lat_copy(0, side).wait_send()

    @pl.when(has_south)
    def _():
        for side in range(3):
            lat_copy(1, side).wait_send()


def step_kernel(rows_total, t_ref, s_ref, u_ref, v_ref, b_ref, mix_ref, wind_ref, halo_ref, part_ref,
                t_out, s_out, u_out, v_out):
    sub = lax.broadcasted_iota(jnp.int32, (C, R), 0)
    lane = lax.broadcasted_iota(jnp.int32, (C, R), 1)
    first_col, last_col = sub == 0, sub == C - 1
    first_row, last_row = lane == 0, lane == R - 1
    south_two, north_two = lane >= R - 2, lane < 2

    def halo(at):
        return jnp.broadcast_to(halo_ref[at : at + 1, :], (C, R))

    def west_of(x, edge):
        return jnp.where(first_col, edge, pltpu.roll(x, 1, 0))

    def east_of(x, edge):
        return jnp.where(last_col, edge, pltpu.roll(x, C - 1, 0))

    south = halo_ref[ROW_S + 1 : ROW_S + 1 + C, :]
    north = halo_ref[ROW_N + 1 : ROW_N + 1 + C, :]

    def south_edge(shifted, at):
        return jnp.where(first_row, pltpu.roll(south, -at % R, 1), shifted)

    def north_edge(shifted, at):
        return jnp.where(last_row, pltpu.roll(north, (R - 1 - at) % R, 1), shifted)

    def south_of(x, at):
        return jnp.where(first_row, pltpu.roll(south, -at % R, 1), pltpu.roll(x, 1, 1))

    def north_of(x, at):
        return jnp.where(last_row, pltpu.roll(north, (R - 1 - at) % R, 1), pltpu.roll(x, R - 1, 1))

    def shifted_south(edge, corner, at):
        spread = lax.broadcasted_iota(jnp.int32, edge.shape, 1)
        return jnp.where(spread == 0, pltpu.roll(corner, -at % R, 1), pltpu.roll(edge, 1, 1))

    def shifted_north(edge, corner, at):
        spread = lax.broadcasted_iota(jnp.int32, edge.shape, 1)
        return jnp.where(spread == R - 1, pltpu.roll(corner, (R - 1 - at) % R, 1),
                         pltpu.roll(edge, R - 1, 1))

    north_west, north_east = halo(ROW_N), halo(ROW_N + C + 1)
    south_east = halo(ROW_S + C + 1)
    b = b_ref[...].astype(jnp.float32)
    bw_edge, be_edge = halo(ROW_W + 97), halo(ROW_E + 96)
    b_w = west_of(b, bw_edge)
    b_e = east_of(b, be_edge)
    b_s = south_of(b, LANE_B + 1)
    b_n = north_of(b, LANE_B)
    b_nn = north_of(b_n, LANE_B + 1)
    b_nw = west_of(b_n, shifted_north(bw_edge, north_west, LANE_B))
    b_ne = east_of(b_n, shifted_north(be_edge, north_east, LANE_B))
    b_se = east_of(b_s, shifted_south(be_edge, south_east, LANE_B + 1))
    least = jnp.minimum
    d_u, d_v = least(b, b_e), least(b, b_n)
    d_vs = least(b, b_s)
    d_un, d_us = least(d_u, least(b_n, b_ne)), least(d_u, least(b_s, b_se))
    v_pairs = (least(d_v, least(b_e, b_ne)), least(d_v, least(b_w, b_nw)), least(d_v, b_nn),
               least(d_v, d_vs))

    base = (lax.axis_index("lat") * R + lane).astype(jnp.float32)
    cor_u = 2.0 * (base + 0.5) / rows_total - 1.0
    cor_v = 2.0 * (base + 1.0) / rows_total - 1.0

    zero = jnp.zeros((C, R), jnp.float32)
    sum_y = zero
    above = zero
    value = [zero] * 4
    outs = (t_out, s_out, u_out, v_out)

    for k in range(K):
        def keep(depth, x):
            return jnp.where(depth > k, x, 0.0)

        u = u_ref[k]
        v = v_ref[k]
        uw_edge = halo(ROW_W + 64 + k)
        vw_edge = halo(ROW_W + 80 + k)
        ve_edge = halo(ROW_E + 80 + k)
        u_s = south_edge(part_ref[SHIFT_U, k], LANE_U + k)
        u_n = north_edge(part_ref[SHIFT_U + 1, k], LANE_U + k)
        v_w = west_of(v, vw_edge)
        v_e = east_of(v, ve_edge)
        v_s = south_edge(part_ref[SHIFT_V, k], LANE_V + k)
        v_n = north_edge(part_ref[SHIFT_V + 1, k], LANE_V + k)

        fy = keep(d_v, v) * (1.0 / 12.0)
        fy_s = keep(d_vs, v_s) * (1.0 / 12.0)

        stars, norths, centres = [], [], []
        for part, shift, ref, first in ((PART_T, SHIFT_T, t_ref, LANE_T),
                                        (PART_S, SHIFT_S, s_ref, LANE_S)):
            c = ref[k]
            at = first + 2 * k
            c_s = south_edge(part_ref[shift, k], at + 1)
            c_ss = jnp.where(north_two, pltpu.roll(south, -at % R, 1), part_ref[shift + 1, k])
            c_n = north_edge(part_ref[shift + 2, k], at)
            c_nn = jnp.where(south_two, pltpu.roll(north, (R - 2 - at) % R, 1),
                             part_ref[shift + 3, k])
            advect = (
                fy_s * (7.0 * (c_s + c) - (c_ss + c_n)) - fy * (7.0 * (c + c_n) - (c_s + c_nn))
            )
            spread = keep(b_n, c_n - c) + keep(b_s, c_s - c)
            stars.append(c + keep(b, TIME_STEP * (part_ref[part, k] + (advect + TRACER_DIFF * spread))))
            centres.append(c)
            norths.append(c_n)

        def buoyancy(depth, pair):
            return keep(depth, THERMAL_EXPANSION * pair[0] - HALINE_CONTRACTION * pair[1])

        here = buoyancy(b, centres)
        step_y = buoyancy(b_n, norths) - here
        sum_y = sum_y + step_y

        pair_v = v + v_s
        edge_v = ve_edge + jnp.where(
            first_row, pltpu.roll(south_east, -(LANE_V + k) % R, 1), halo(ROW_VS + k))
        v_at_u = 0.25 * (pair_v + east_of(pair_v, edge_v))
        pair_u = u + u_n
        edge_u = uw_edge + jnp.where(
            last_row, pltpu.roll(north_west, (R - 1 - LANE_U - k) % R, 1), halo(ROW_UN + k))
        u_at_v = 0.25 * (pair_u + west_of(pair_u, edge_u))
        u_visc = part_ref[PART_U, k] + (keep(d_un, u_n - u) + keep(d_us, u_s - u))
        v_visc = (keep(v_pairs[0], v_e - v) + keep(v_pairs[1], v_w - v)) + (
            keep(v_pairs[2], v_n - v) + keep(v_pairs[3], v_s - v))
        u_star = u + TIME_STEP * (
            cor_u * v_at_u - part_ref[PART_P, k] + MOMENTUM_VISC * u_visc)
        v_star = v + TIME_STEP * (
            -cor_v * u_at_v - (sum_y - 0.5 * step_y) + MOMENTUM_VISC * v_visc)
        if k == 0:
            u_star = u_star + TIME_STEP * WIND_GAIN * wind_ref[0]
            v_star = v_star + TIME_STEP * WIND_GAIN * wind_ref[1]
        coupling = zero if k == K - 1 else jnp.where(b > k + 1, TIME_STEP * mix_ref[k], 0.0)
        inv = part_ref[PART_INV, k]
        for index in range(2):
            value[index] = (stars[index] + above * value[index]) * inv
            outs[index][k] = value[index]
        above = coupling
        for index, depth, star in ((2, d_u, u_star), (3, d_v, v_star)):
            if k > 0:
                star = star + DRAG * value[index]
            if k < K - 1:
                star = star * jnp.where(depth > k + 1, INNER[k], LAST[k])
            else:
                star = star * LAST[k]
            value[index] = keep(depth, star)
            outs[index][k] = value[index]

    result = list(value)
    for k in range(K - 2, -1, -1):
        for index in range(4):
            if index < 2:
                result[index] = outs[index][k] - part_ref[PART_RATIO, k] * result[index]
            else:
                result[index] = outs[index][k] + (DRAG * INNER[k]) * result[index]
            outs[index][k] = result[index]


def shards(thermal_anomaly, saltiness_anomaly, zonal_current, meridional_current,
           bottom_ocean_layer, seam_axis_meridian, interface_diffusivity, atmospheric_forcing):
    n_lon = lax.axis_size("lon")
    n_lat = lax.axis_size("lat")
    n_y = 8 if n_lon >= 64 else n_lon // 2
    n_g = n_lon // n_y
    fields = (thermal_anomaly, saltiness_anomaly, zonal_current, meridional_current)
    vmem = pl.BlockSpec(memory_space=pltpu.VMEM)
    f32 = jnp.float32

    def exchange_body(*refs):
        exchange_kernel(n_lon, n_lat, n_y, *refs)

    def step_body(*refs):
        step_kernel(R * n_lat, *refs)

    halo, part = pl.pallas_call(
        exchange_body,
        name="exchange",
        out_shape=(jax.ShapeDtypeStruct((HALO_ROWS, R), f32),
                   jax.ShapeDtypeStruct((PARTS, K, C, R), f32)),
        in_specs=[pl.BlockSpec(memory_space=pltpu.HBM)] * 7,
        out_specs=(vmem, vmem),
        scratch_shapes=[
            pltpu.SMEM((1,), jnp.int32),
            *[pltpu.VMEM((K * C, R), f32) for _ in range(4)],
            pltpu.VMEM((C, R), jnp.int32),
            pltpu.VMEM((K - 1, C, R), f32),
            pltpu.VMEM((2, LON_ROWS, R), f32),
            pltpu.VMEM((2, LON_ROWS, R), f32),
            pltpu.VMEM((2, C, R), f32),
            pltpu.VMEM((6, C, R), f32),
            pltpu.VMEM((n_y * C, R), f32),
            pltpu.VMEM((n_g * 16, R), f32),
            pltpu.SemaphoreType.DMA((7,)),
            pltpu.SemaphoreType.DMA((2, 2)),
            pltpu.SemaphoreType.DMA((2, 6)),
            pltpu.SemaphoreType.DMA((2, n_y - 1)),
            pltpu.SemaphoreType.DMA((2, n_g - 1)),
        ],
        compiler_params=pltpu.CompilerParams(collective_id=0, has_side_effects=True,
                                             vmem_limit_bytes=4 << 20),
    )(seam_axis_meridian, *[
        pltpu.with_memory_space_constraint(operand, pltpu.HBM)
        for operand in (*[field.reshape(K * C, R) for field in fields], bottom_ocean_layer,
                        interface_diffusivity)
    ])
    return pl.pallas_call(
        step_body,
        name="step",
        out_shape=tuple(jax.ShapeDtypeStruct((K, C, R), f32) for _ in range(4)),
        in_specs=[vmem] * 9,
        out_specs=(vmem,) * 4,
        compiler_params=pltpu.CompilerParams(vmem_limit_bytes=4 << 20),
    )(*[pltpu.with_memory_space_constraint(operand, pltpu.HBM)
        for operand in (*fields, bottom_ocean_layer, interface_diffusivity, atmospheric_forcing)],
      halo, part)


def solution(mesh):
    grid = P(None, "lon", "lat")
    return jax.shard_map(
        shards,
        mesh=mesh,
        in_specs=(grid, grid, grid, grid, P("lon", "lat"), P(), grid, grid),
        out_specs=(grid,) * 4,
        check_vma=False,
    )
```
